512 devices in a mesh: path: 2 (over core), lon: 32 (over z_hi, x, y), lat: 8 (over z_lo).
Axes of the slice: x: 4, y: 4, z: 16 (z_hi: 2, z_lo: 8; z = z_hi * 8 + z_lo), core: 2. Of those that a mesh axis runs over, the one named last changes fastest.
Arguments:
- observed: bfloat16 [512, 128, 384], P('lon', 'lat'), may hold values from -6 to 6
- baseline: bfloat16 [512, 128, 384], P('lon', 'lat'), may hold values from -6 to 6
- cotangent: bfloat16 [512, 128, 384], P('lon', 'lat'), may hold values from -6 to 6
- first_weight: bfloat16 [9, 384, 384], P(None, 'path'), may hold values from -0.109375 to 0.109375
- first_bias: float32 [384], replicated, may hold values from -3 to 3
- second_weight: bfloat16 [9, 384, 384], P(None, 'path'), may hold values from -0.109375 to 0.109375
- second_bias: float32 [384], replicated, may hold values from -3 to 3
Outputs:
- attribution: bfloat16 [512, 128, 384], P(('lon', 'path'), 'lat')
The draws below stay inside these ranges and needn't reach their ends.
All inputs are finite; a program needn't handle non-finite values.
Results may differ from the reference program's by a relative error of at most 0.0038.
Values may be sent and summed in bfloat16 or wider, within the bound.
A program may use at most 64 MiB of HBM per device.

```python
import jax
import jax.numpy as jnp

C = 384
NEAR = 4
FAR = 16
NLON = 512
NLAT = 128
N_PATH = 2


def block_levels(key, extent, split, least, high):
    def one(dim, shards_of):
        draws = jax.random.uniform(jax.random.fold_in(jax.random.fold_in(key, 6), dim), (shards_of,), jnp.float32, least / len(split), high / len(split))
        return jnp.repeat(jnp.exp(draws), extent[dim] // shards_of).reshape((-1,) + (1,) * (len(extent) - dim - 1))

    loudness = one(*split[0])
    for cut in split[1:]:
        loudness = loudness * one(*cut)
    return loudness


def bell_draw(rng, dims, deviation, most, cuts=(), held_as=jnp.bfloat16):
    gain = block_levels(rng, dims, cuts, -0.22, 0.18) if cuts else 1.0
    values = jax.random.normal(rng, dims, jnp.float32) * deviation * gain
    return jnp.minimum(jnp.maximum(values, -most), most).astype(held_as)


def setup_inputs(seed: int = 0) -> dict:
    key_list = jax.random.split(jax.random.key(seed), 8)
    observed = bell_draw(key_list[0], (NLON, NLAT, C), 1.0, 6.0, ((0, 32), (1, 8)))
    baseline = bell_draw(key_list[1], (NLON, NLAT, C), 1.0, 6.0, ((0, 32), (1, 8)))
    cotangent = bell_draw(key_list[2], (NLON, NLAT, C), 1.0, 6.0, ((0, 32), (1, 8)))
    first_weight = bell_draw(key_list[3], (9, C, C), (9 * C) ** -0.5, 0.109375, ((1, 2),))
    first_bias = bell_draw(key_list[4], (C,), 0.5, 3.0, (), jnp.float32)
    second_weight = bell_draw(key_list[5], (9, C, C), (9 * C) ** -0.5, 0.109375, ((1, 2),))
    second_bias = bell_draw(key_list[6], (C,), 0.5, 3.0, (), jnp.float32)
    return {"observed": observed, "baseline": baseline, "cotangent": cotangent, "first_weight": first_weight, "first_bias": first_bias, "second_weight": second_weight, "second_bias": second_bias}


def smooth_act(value):
    return jax.nn.gelu(value, approximate=True)

def act_adjoint(pre_value, upstream):
    unused, pullback = jax.vjp(smooth_act, pre_value)
    return pullback(upstream)[0]

def stencil(field, weights, dilation, forward):
    rows, cols = (field.shape[0], field.shape[1])
    padded = jnp.pad(field, ((dilation, dilation), (dilation, dilation), (0, 0)))
    accumulated = jnp.zeros((rows, cols, weights.shape[1]), jnp.float32)
    for offset_row in (-1, 0, 1):
        for offset_col in (-1, 0, 1):
            tap_index = (offset_row + 1) * 3 + offset_col + 1
            sign = 1 if forward else -1
            start_row = dilation + sign * offset_row * dilation
            start_col = dilation + sign * offset_col * dilation
            window = padded[start_row:start_row + rows, start_col:start_col + cols, :].astype(jnp.float32)
            kernel = weights[tap_index].astype(jnp.float32)
            if forward:
                accumulated = accumulated + jnp.einsum('lmc,co->lmo', window, kernel)
            else:
                accumulated = accumulated + jnp.einsum('lmo,co->lmc', window, kernel)
    return accumulated

def reference(observed, baseline, cotangent, first_weight, first_bias, second_weight, second_bias):
    diff = observed.astype(jnp.float32) - baseline.astype(jnp.float32)
    upstream = cotangent.astype(jnp.float32)
    grad_sum = jnp.zeros(diff.shape, jnp.float32)
    for point in range(N_PATH):
        mix_weight = (point + 0.5) / N_PATH
        point_field = (baseline.astype(jnp.float32) + mix_weight * diff).astype(jnp.bfloat16)
        first_pre = stencil(point_field, first_weight, NEAR, True) + first_bias
        hidden = (point_field.astype(jnp.float32) + smooth_act(first_pre)).astype(jnp.bfloat16)
        second_pre = stencil(hidden, second_weight, FAR, True) + second_bias
        second_adj = act_adjoint(second_pre, upstream).astype(jnp.bfloat16)
        hidden_adj = upstream + stencil(second_adj, second_weight, FAR, False)
        first_adj = act_adjoint(first_pre, hidden_adj).astype(jnp.bfloat16)
        point_grad = hidden_adj + stencil(first_adj, first_weight, NEAR, False)
        grad_sum = grad_sum + point_grad
    return (diff * grad_sum / N_PATH).astype(jnp.bfloat16)
```

```python
import functools

import jax
import jax.numpy as jnp
import numpy as np
from jax import lax
from jax.experimental import pallas as pl
from jax.experimental.pallas import tpu as pltpu
from jax.sharding import PartitionSpec as P

MESH = pl.DeviceIdType.MESH
F32 = jnp.float32
BF16 = jnp.bfloat16
C = 384
T = 16


def one_hot(rows, cols, pairs):
    out = np.zeros((rows, cols), np.float32)
    for r, c in pairs:
        out[r, c] = 1.0
    return out


def moves():
    split = one_hot(256, 256, [
        ((4 * s + c) * 16 + 4 * k + q, (4 * k + c) * 16 + 4 * q + s)
        for s in range(4) for c in range(4) for k in range(4) for q in range(4)])
    edges = one_hot(128, 256, [(m, 4 * m) for m in range(64)] + [(64 + m, 4 * m + 3) for m in range(64)])
    minus, plus = [], []
    for m in range(-4, 68):
        for q in range(4):
            f = 4 * (m + 4) + q
            outer_l = 16 + m if 0 <= m < 64 else (4 * (m + 4) + 3 if m < 0 else 80 + 4 * (m - 64) + 3)
            outer_r = 16 + m if 0 <= m < 64 else (4 * (m + 4) if m < 0 else 80 + 4 * (m - 64))
            minus.append((f, f - 1 if q else 288 + outer_l))
            plus.append((f, f + 1 if q < 3 else 288 + outer_r))
    minus = one_hot(288, 384, minus)
    plus = one_hot(288, 384, plus)
    join = one_hot(128, 128, [
        ((4 * k + c) * 16 + 4 * q + s, (4 * s + c) * 8 + 4 * k + q)
        for s in range(4) for c in range(4) for k in range(2) for q in range(4)])
    return [jnp.asarray(v, BF16) for v in (split, edges, minus, plus, join)]


def dot(a, b):
    return lax.dot_general(a, b, (((1,), (0,)), ((), ())), preferred_element_type=F32)


def dot_t(a, b):
    return lax.dot_general(a, b, (((1,), (1,)), ((), ())), preferred_element_type=F32)


ROOT = 0.7978845608028654


def gelu_parts(x):
    square = x * x
    t = jnp.tanh(ROOT * (x + 0.044715 * (x * square)))
    half = 0.5 * (1.0 + t)
    slope = half + 0.5 * x * (1.0 - t * t) * (ROOT * (1.0 + 3 * 0.044715 * square))
    return x * half, slope


def kernel(obs_h, base_h, cot_h, w1_h, b1_ref, w2_h, b2_ref, split_ref, edges_ref, minus_ref, plus_ref, join_ref,
           out_ref,
           obs, base, cot, snd, w1, w2, x, ct, h, hl, hr, a, al, ar, f, nl, nr, ml, mr, pk, qs, pre, slope, adj,
           psum_in, back,
           ls, ws, wr, as_, ar_, es, er, ps, pr, os_, or_):
    p = lax.axis_index("path")
    lon = lax.axis_index("lon")
    lat = lax.axis_index("lat")
    me = lon % T
    zhi = lon // T
    far = (lon + T) % (2 * T)
    has_l = lat > 0
    has_r = lat < 7

    loads = [pltpu.make_async_copy(src, dst, ls.at[i]) for i, (src, dst) in enumerate(
        ((obs_h, obs), (base_h, base), (cot_h, cot)))]
    for copy in loads:
        copy.start()
    half = pl.ds(pl.multiple_of(p * 192, 64), 192)
    own_w = [pltpu.make_async_copy(src, dst.at[:, half, :], ls.at[3 + i]) for i, (src, dst) in enumerate(
        ((w1_h, w1), (w2_h, w2)))]
    for copy in own_w:
        copy.start()

    barrier = pltpu.get_barrier_semaphore()

    def greet(**where):
        pl.semaphore_signal(barrier, inc=1, device_id=where, device_id_type=MESH)

    for o in range(1, T):
        greet(lon=zhi * T + (me + o) % T)
    greet(lon=far)
    greet(path=1 - p)

    @pl.when(has_l)
    def _():
        greet(lat=lat - 1)

    @pl.when(has_r)
    def _():
        greet(lat=lat + 1)

    blank = jnp.zeros((16, C), BF16)
    side = jnp.where(zhi == 0, 0, 17)
    for ref in (x, f, h, hl, hr, a, al, ar):
        ref[side] = blank
    nside = jnp.where(zhi == 0, 0, 5)
    for ref in (nl, nr, ml, mr):
        ref[nside] = blank

    @pl.when(jnp.logical_not(has_l))
    def _():
        for ref in (hl, al, nl, ml):
            ref[...] = jnp.zeros(ref.shape, BF16)

    @pl.when(jnp.logical_not(has_r))
    def _():
        for ref in (hr, ar, nr, mr):
            ref[...] = jnp.zeros(ref.shape, BF16)

    for copy in loads:
        copy.wait()
    low = base[...].astype(F32)
    mix = (p.astype(F32) + 0.5) / 2
    field = (low + mix * (obs[...].astype(F32) - low)).astype(BF16)
    snd[0] = dot(split_ref[...], field.reshape(256, C)).astype(BF16).reshape(T, 16, C)
    snd[1] = dot(split_ref[...], cot[...].reshape(256, C)).astype(BF16).reshape(T, 16, C)

    pl.semaphore_wait(barrier, 17 + has_l.astype(jnp.int32) + has_r.astype(jnp.int32))

    def spread(which, dst, o):
        d = (me + o) % T
        return pltpu.make_async_remote_copy(
            src_ref=snd.at[which, d], dst_ref=dst, send_sem=as_.at[which, o], recv_sem=ar_.at[which, o],
            device_id={"lon": zhi * T + d}, device_id_type=MESH)

    for o in range(1, T):
        spread(0, x.at[1 + me], o).start()
    push_w = [pltpu.make_async_remote_copy(
        src_ref=src, dst_ref=dst.at[:, half, :], send_sem=ws.at[i], recv_sem=wr.at[i],
        device_id={"path": 1 - p}, device_id_type=MESH) for i, (src, dst) in enumerate(((w1_h, w1), (w2_h, w2)))]
    push_w[0].start()
    for o in range(1, T):
        spread(1, ct.at[me], o).start()
    push_w[1].start()
    x[1 + me] = snd[0, me]
    ct[me] = snd[1, me]

    fs = jnp.where(zhi == 0, 16, 1)
    fd = jnp.where(zhi == 0, 0, 17)
    fr = jnp.where(zhi == 0, 17, 0)
    nf = jnp.where(zhi == 0, 5, 0)

    def send(stage, slot, src, dst, **where):
        return pltpu.make_async_remote_copy(
            src_ref=src, dst_ref=dst, send_sem=es.at[stage, slot], recv_sem=er.at[stage, slot],
            device_id=where, device_id_type=MESH)

    def exchange(stage, main, left, right, left_src, right_src, body, edge):
        to_far = send(stage, 2, main.at[fs], main.at[fd], lon=far)
        to_far.start()
        from_far = send(stage, 2, main.at[fs], main.at[fr], lon=far)

        def right_going():
            return [send(stage, 0, right_src, left.at[body], lat=lat + 1),
                    send(stage, 3, main.at[fr], left.at[edge], lat=lat + 1)]

        def left_going():
            return [send(stage, 1, left_src, right.at[body], lat=lat - 1),
                    send(stage, 4, main.at[fr], right.at[edge], lat=lat - 1)]

        @pl.when(has_r)
        def _():
            right_going()[0].start()

        @pl.when(has_l)
        def _():
            left_going()[0].start()

        from_far.wait_recv()

        @pl.when(has_r)
        def _():
            right_going()[1].start()

        @pl.when(has_l)
        def _():
            left_going()[1].start()

        @pl.when(has_l)
        def _():
            for copy in right_going():
                copy.wait_recv()

        @pl.when(has_r)
        def _():
            for copy in left_going():
                copy.wait_recv()

        def finish():
            to_far.wait_send()

            @pl.when(has_r)
            def _():
                for copy in right_going():
                    copy.wait_send()

            @pl.when(has_l)
            def _():
                for copy in left_going():
                    copy.wait_send()

        return finish

    inner = pl.ds(1, 16)

    def near_exchange(stage, main, left, right):
        pk[stage] = dot(edges_ref[...], main[inner].reshape(256, C)).astype(BF16).reshape(8, 16, C)
        return exchange(stage, main, left, right, pk.at[stage, pl.ds(0, 4)], pk.at[stage, pl.ds(4, 4)],
                        pl.ds(1, 4), nf)

    def near_windows(main, left, right):
        whole = main[...].reshape(288, C)
        qs[1] = whole.astype(F32)
        for j, move, outer in ((0, minus_ref, left), (2, plus_ref, right)):
            qs[j] = dot(move[:, :288], whole) + dot(move[:, 288:], outer[...].reshape(96, C))

    def near_conv(weights, forward):
        total = jnp.zeros((256, C), F32)
        for i in (-1, 0, 1):
            for j in (-1, 0, 1):
                sign = 1 if forward else -1
                window = qs[1 + sign * j, pl.ds(16 + 4 * sign * i, 256), :].astype(BF16)
                total = total + (dot if forward else dot_t)(window, weights[3 * (i + 1) + j + 1])
        return total

    def far_conv(parts, weights, forward):
        total = jnp.zeros((256, C), F32)
        for i in (-1, 0, 1):
            for j in (-1, 0, 1):
                sign = 1 if forward else -1
                window = parts[1 + sign * j][pl.ds(1 + sign * i, 16)].reshape(256, C)
                total = total + (dot if forward else dot_t)(window, weights[3 * (i + 1) + j + 1])
        return total

    for o in range(1, T):
        s = (me + T - o) % T
        pltpu.make_async_remote_copy(
            src_ref=snd.at[0, 0], dst_ref=x.at[1 + s], send_sem=as_.at[0, o], recv_sem=ar_.at[0, o],
            device_id={"lon": zhi * T + s}, device_id_type=MESH).wait_recv()

    done = [near_exchange(0, x, nl, nr)]
    near_windows(x, nl, nr)
    own_w[0].wait()
    push_w[0].wait_recv()
    act, der = gelu_parts(near_conv(w1, True) + b1_ref[...])
    slope[...] = der
    h[inner] = (x[inner].reshape(256, C).astype(F32) + act).astype(BF16).reshape(16, 16, C)

    done.append(exchange(1, h, hl, hr, h.at[inner], h.at[inner], inner, fr))
    own_w[1].wait()
    push_w[1].wait_recv()
    for o in range(1, T):
        s = (me + T - o) % T
        pltpu.make_async_remote_copy(
            src_ref=snd.at[1, 0], dst_ref=ct.at[s], send_sem=as_.at[1, o], recv_sem=ar_.at[1, o],
            device_id={"lon": zhi * T + s}, device_id_type=MESH).wait_recv()
    up = ct[...].reshape(256, C).astype(F32)
    _, der = gelu_parts(far_conv((hl, h, hr), w2, True) + b2_ref[...])
    a[inner] = (der * up).astype(BF16).reshape(16, 16, C)

    done.append(exchange(2, a, al, ar, a.at[inner], a.at[inner], inner, fr))
    hidden_adj = ct[...].reshape(256, C).astype(F32) + far_conv((al, a, ar), w2, False)
    adj[...] = hidden_adj
    f[inner] = (slope[...] * hidden_adj).astype(BF16).reshape(16, 16, C)

    done.append(near_exchange(3, f, ml, mr))
    near_windows(f, ml, mr)
    grad = adj[...] + near_conv(w1, False)
    pre[...] = grad.reshape(16, 2, 8, C)

    swap = pltpu.make_async_remote_copy(
        src_ref=pre.at[:, 1 - p], dst_ref=psum_in, send_sem=ps, recv_sem=pr,
        device_id={"path": 1 - p}, device_id_type=MESH)
    swap.start()
    swap.wait()
    pre[:, p] = pre[:, p] + psum_in[...]

    def collect(o):
        d = (me + o) % T
        return pltpu.make_async_remote_copy(
            src_ref=pre.at[d, p], dst_ref=back.at[me], send_sem=os_.at[o], recv_sem=or_.at[o],
            device_id={"lon": zhi * T + d}, device_id_type=MESH)

    for o in range(1, T):
        collect(o).start()
    back[me] = pre[me, p]
    for finish in done:
        finish()
    for o in range(1, T):
        for which in (0, 1):
            spread(which, x.at[1 + me] if which == 0 else ct.at[me], o).wait_send()
    for copy in push_w:
        copy.wait_send()
    for o in range(1, T):
        s = (me + T - o) % T
        pltpu.make_async_remote_copy(
            src_ref=pre.at[0, 0], dst_ref=back.at[s], send_sem=os_.at[o], recv_sem=or_.at[o],
            device_id={"lon": zhi * T + s}, device_id_type=MESH).wait_recv()
    got = back[...].reshape(128, C)
    top = got.astype(BF16)
    rest = (got - top.astype(F32)).astype(BF16)
    total = dot(join_ref[...], top) + dot(join_ref[...], rest)
    rows = pl.ds(p * 8, 8)
    diff = obs[rows].astype(F32) - base[rows].astype(F32)
    out_ref[...] = (diff * total.reshape(8, 16, C) / 2).astype(BF16)
    for o in range(1, T):
        collect(o).wait_send()


def shards(observed, baseline, cotangent, first_weight, first_bias, second_weight, second_bias):
    hbm = pl.BlockSpec(memory_space=pl.ANY)
    vmem = pl.BlockSpec(memory_space=pltpu.VMEM)
    block = pltpu.VMEM((16, 16, C), BF16)
    ext = pltpu.VMEM((18, 16, C), BF16)
    edge = pltpu.VMEM((6, 16, C), BF16)
    dma = pltpu.SemaphoreType.DMA
    return pl.pallas_call(
        kernel,
        out_shape=jax.ShapeDtypeStruct((8, 16, C), BF16),
        in_specs=[hbm, hbm, hbm, hbm, vmem, hbm, vmem] + [vmem] * 5,
        out_specs=vmem,
        scratch_shapes=[
            block, block, block, pltpu.VMEM((2, 16, 16, C), BF16),
            pltpu.VMEM((9, C, C), BF16), pltpu.VMEM((9, C, C), BF16),
            ext, block, ext, ext, ext, ext, ext, ext, ext, edge, edge, edge, edge,
            pltpu.VMEM((4, 8, 16, C), BF16),
            pltpu.VMEM((3, 288, C), F32),
            pltpu.VMEM((16, 2, 8, C), F32),
            pltpu.VMEM((256, C), F32), pltpu.VMEM((256, C), F32),
            pltpu.VMEM((16, 8, C), F32), pltpu.VMEM((16, 8, C), F32),
            dma((5,)), dma((2,)), dma((2,)), dma((2, T)), dma((2, T)), dma((4, 5)), dma((4, 5)),
            dma, dma, dma((T,)), dma((T,)),
        ],
        compiler_params=pltpu.CompilerParams(collective_id=0, has_side_effects=True),
    )(observed, baseline, cotangent, first_weight, first_bias.reshape(1, C), second_weight,
      second_bias.reshape(1, C), *moves())


def solution(mesh):
    placed = (
        P("lon", "lat", None),
        P("lon", "lat", None),
        P("lon", "lat", None),
        P(None, "path", None),
        P(),
        P(None, "path", None),
        P(),
    )
    return jax.shard_map(
        shards,
        mesh=mesh,
        in_specs=placed,
        out_specs=P(("lon", "path"), "lat", None),
        check_vma=False,
    )
```

```python
import functools

import jax
import jax.numpy as jnp
import numpy as np
from jax import lax
from jax.experimental import pallas as pl
from jax.experimental.pallas import tpu as pltpu
from jax.sharding import PartitionSpec as P

MESH = pl.DeviceIdType.MESH
F32 = jnp.float32
BF16 = jnp.bfloat16
C = 384
T = 16


def one_hot(rows, cols, pairs):
    out = np.zeros((rows, cols), np.float32)
    for r, c in pairs:
        out[r, c] = 1.0
    return out


def moves():
    split = one_hot(256, 256, [
        ((4 * s + c) * 16 + 4 * k + q, (4 * k + c) * 16 + 4 * q + s)
        for s in range(4) for c in range(4) for k in range(4) for q in range(4)])
    edges = one_hot(128, 256, [(m, 4 * m) for m in range(64)] + [(64 + m, 4 * m + 3) for m in range(64)])
    edges_far = one_hot(32, 48, [(m, 4 * m) for m in range(12)] + [(16 + m, 4 * m + 3) for m in range(12)])

    def shift(rows, total, step):
        edge = 0 if step < 0 else 3
        return one_hot(4 * rows, total, [
            (4 * m + q, 4 * rows + m if q == edge else 4 * m + q + step) for m in range(rows) for q in range(4)])

    join = one_hot(128, 128, [
        ((4 * k + c) * 16 + 4 * q + s, (4 * s + c) * 8 + 4 * k + q)
        for s in range(4) for c in range(4) for k in range(2) for q in range(4)])
    return [jnp.asarray(v, BF16) for v in (
        split, edges, edges_far, shift(64, 320, -1), shift(64, 320, 1), shift(12, 64, -1), shift(12, 64, 1), join)]


def dot(a, b):
    return lax.dot_general(a, b, (((1,), (0,)), ((), ())), preferred_element_type=F32)


def dot_t(a, b):
    return lax.dot_general(a, b, (((1,), (1,)), ((), ())), preferred_element_type=F32)


ROOT = 0.7978845608028654


def gelu_parts(x):
    square = x * x
    t = jnp.tanh(ROOT * (x + 0.044715 * (x * square)))
    half = 0.5 * (1.0 + t)
    slope = half + 0.5 * x * (1.0 - t * t) * (ROOT * (1.0 + 3 * 0.044715 * square))
    return x * half, slope


def kernel(obs_h, base_h, cot_h, w1_h, b1_ref, w2_h, b2_ref, split_ref, edges_ref, edges_far_ref,
           minus_ref, plus_ref, minus_far_ref, plus_far_ref, join_ref,
           out_ref,
           obs, base, cot, snd, w1, w2, x, ct, h, hl, hr, a, al, ar, f, nl, nr, ml, mr, pk, pkf, hop, hop_ct,
           qs, qf, slope, adj, pre, psum_in, back,
           ls, ws, wr, as_, ar_, es, er, fs, fr, ps, pr, os_, or_):
    p = lax.axis_index("path")
    lon = lax.axis_index("lon")
    lat = lax.axis_index("lat")
    me = lon % T
    zhi = lon // T
    z = zhi * 8 + lat
    has_l = lat > 0
    has_r = lat < 7

    def along(step):
        there = (z + step + 16) % 16
        return {"lon": (there // 8) * T + me, "lat": there % 8}

    loads = [pltpu.make_async_copy(src, dst, ls.at[i]) for i, (src, dst) in enumerate(
        ((obs_h, obs), (base_h, base), (cot_h, cot)))]
    for copy in loads:
        copy.start()
    half = pl.ds(pl.multiple_of(p * 192, 64), 192)
    own_w = [pltpu.make_async_copy(src, dst.at[:, half, :], ls.at[3 + i]) for i, (src, dst) in enumerate(
        ((w1_h, w1), (w2_h, w2)))]
    for copy in own_w:
        copy.start()

    barrier = pltpu.get_barrier_semaphore()

    def greet(**where):
        pl.semaphore_signal(barrier, inc=1, device_id=where, device_id_type=MESH)

    for o in range(1, T):
        greet(lon=zhi * T + (me + o) % T)
    greet(path=1 - p)
    greet(**along(4))
    greet(**along(-4))

    @pl.when(has_l)
    def _():
        greet(lat=lat - 1)

    @pl.when(has_r)
    def _():
        greet(lat=lat + 1)

    outside = 2 + 17 * zhi
    past = 19 * (1 - zhi)
    blank = jnp.zeros((16, C), BF16)
    for ref in (h, hl, hr, a, al, ar):
        ref[outside] = blank
    for ref in (nl, nr, ml, mr):
        ref[0] = blank
        ref[5] = blank
    for t in (0, 1, 2, 19, 20, 21):
        f[t] = blank
    for j in range(3):
        qs[j, :64] = jnp.zeros((64, C), F32)
        qs[j, 320:] = jnp.zeros((64, C), F32)

    @pl.when(jnp.logical_not(has_l))
    def _():
        for ref in (hl, al, nl, ml):
            ref[...] = jnp.zeros(ref.shape, BF16)

    @pl.when(jnp.logical_not(has_r))
    def _():
        for ref in (hr, ar, nr, mr):
            ref[...] = jnp.zeros(ref.shape, BF16)

    for copy in loads:
        copy.wait()
    low = base[...].astype(F32)
    mix = (p.astype(F32) + 0.5) / 2
    field = (low + mix * (obs[...].astype(F32) - low)).astype(BF16)
    snd[0] = dot(split_ref[...], field.reshape(256, C)).astype(BF16).reshape(T, 16, C)
    snd[1] = dot(split_ref[...], cot[...].reshape(256, C)).astype(BF16).reshape(T, 16, C)

    pl.semaphore_wait(barrier, 18 + has_l.astype(jnp.int32) + has_r.astype(jnp.int32))

    def remote(src, dst, send_sem, recv_sem, where):
        return pltpu.make_async_remote_copy(
            src_ref=src, dst_ref=dst, send_sem=send_sem, recv_sem=recv_sem, device_id=where, device_id_type=MESH)

    def spread(which, o):
        d = (me + o) % T
        dst = (x, ct)[which].at[3 + me]
        return remote(snd.at[which, d], dst, as_.at[which, o], ar_.at[which, o], {"lon": zhi * T + d})

    def gathered(which, o):
        s = (me + T - o) % T
        dst = (x, ct)[which].at[3 + s]
        return remote(snd.at[which, s], dst, as_.at[which, o], ar_.at[which, o], {"lon": zhi * T + s})

    for o in range(1, T):
        spread(0, o).start()
    push_w = [remote(src, dst.at[:, half, :], ws.at[i], wr.at[i], {"path": 1 - p})
              for i, (src, dst) in enumerate(((w1_h, w1), (w2_h, w2)))]
    push_w[0].start()
    for o in range(1, T):
        spread(1, o).start()
    push_w[1].start()
    x[3 + me] = snd[0, me]
    ct[3 + me] = snd[1, me]

    def first_hop(slot):
        base_x, base_c = 16 - 13 * zhi, 17 - 14 * zhi
        src = (x.at[pl.ds(base_x, 2)], x.at[pl.ds(base_x + 2, 1)],
               ct.at[pl.ds(base_c, 1)], ct.at[pl.ds(base_c + 1, 1)])[slot]
        dst = (hop.at[pl.ds(0, 2)], hop.at[pl.ds(2, 1)], hop_ct.at[pl.ds(0, 1)], hop_ct.at[pl.ds(1, 1)])[slot]
        return remote(src, dst, fs.at[slot], fr.at[slot], along(-4 if slot % 2 else 4))

    def second_hop(slot, coming):
        if coming:
            side = 1 - zhi
        else:
            side = ((z + (4 if slot % 2 else -4) + 16) % 16) // 8
        base_x, base_c = 19 * side, 1 + 18 * side
        src = (hop.at[pl.ds(0, 2)], hop.at[pl.ds(2, 1)], hop_ct.at[pl.ds(0, 1)], hop_ct.at[pl.ds(1, 1)])[slot]
        dst = (x.at[pl.ds(base_x, 2)], x.at[pl.ds(base_x + 2, 1)],
               ct.at[pl.ds(base_c, 1)], ct.at[pl.ds(base_c + 1, 1)])[slot]
        return remote(src, dst, fs.at[4 + slot], fr.at[4 + slot], along(-4 if slot % 2 else 4))

    def right_going(stage, src, dst):
        return remote(src, dst, es.at[stage, 0], er.at[stage, 0], {"lat": lat + 1})

    def left_going(stage, src, dst):
        return remote(src, dst, es.at[stage, 1], er.at[stage, 1], {"lat": lat - 1})

    sent = []

    def give(stage, left_src, right_src, at_left, at_right):
        @pl.when(has_r)
        def _():
            right_going(stage, right_src, at_left).start()

        @pl.when(has_l)
        def _():
            left_going(stage, left_src, at_right).start()

        sent.append((stage, left_src, right_src, at_left, at_right))

    def take(stage):
        left_src, right_src, at_left, at_right = next(v[1:] for v in sent if v[0] == stage)

        @pl.when(has_l)
        def _():
            right_going(stage, right_src, at_left).wait_recv()

        @pl.when(has_r)
        def _():
            left_going(stage, left_src, at_right).wait_recv()

    def give_block(stage, main, left, right, start, count):
        window = pl.ds(start, count)
        give(stage, main.at[window], main.at[window], left.at[window], right.at[window])

    inner = pl.ds(3, 16)
    beyond = pl.ds(past, 3)
    edge = 5 * (1 - zhi)

    def give_edges(stage, main, left, right, layer):
        pk[layer] = dot(edges_ref[...], main[inner].reshape(256, C)).astype(BF16).reshape(8, 16, C)
        give(stage, pk.at[layer, pl.ds(0, 4)], pk.at[layer, pl.ds(4, 4)], left.at[pl.ds(1, 4)], right.at[pl.ds(1, 4)])

    def give_far_edges(stage, main, left, right, layer):
        pkf[layer] = dot(edges_far_ref[...], main[beyond].reshape(48, C)).astype(BF16).reshape(2, 16, C)
        give(stage, pkf.at[layer, pl.ds(0, 1)], pkf.at[layer, pl.ds(1, 1)],
             left.at[pl.ds(edge, 1)], right.at[pl.ds(edge, 1)])

    far_rows = pl.ds(pl.multiple_of(16 * (1 + past), 16), 48)

    def centre(main):
        qs[1, 64:320] = main[inner].reshape(256, C).astype(F32)

    def centre_far(main):
        qs[1, far_rows] = main[beyond].reshape(48, C).astype(F32)

    def sides(main, left, right):
        whole = main[inner].reshape(256, C)
        for j, move, outer in ((0, minus_ref, left), (2, plus_ref, right)):
            qs[j, 64:320] = dot(move[:, :256], whole) + dot(move[:, 256:], outer[pl.ds(1, 4)].reshape(64, C))

    def sides_far(main, left, right):
        whole = main[beyond].reshape(48, C)
        for j, move, outer in ((0, minus_far_ref, left), (2, plus_far_ref, right)):
            qs[j, far_rows] = dot(move[:, :48], whole) + dot(move[:, 48:], outer[edge])

    def near_conv(ref, first, rows, weights, forward, columns):
        total = jnp.zeros((rows, C), F32)
        sign = 1 if forward else -1
        for j in columns:
            for i in (-1, 0, 1):
                window = ref[1 + sign * j, pl.ds(first + 4 * sign * i, rows), :].astype(BF16)
                total = total + (dot if forward else dot_t)(window, weights[3 * (i + 1) + j + 1])
        return total

    def far_conv(parts, start, count, weights, forward):
        total = jnp.zeros((16 * count, C), F32)
        sign = 1 if forward else -1
        for j in (0, -1, 1):
            for i in (-1, 0, 1):
                window = parts[1 + sign * j][pl.ds(start + sign * i, count)].reshape(16 * count, C)
                total = total + (dot if forward else dot_t)(window, weights[3 * (i + 1) + j + 1])
        return total

    for o in range(1, T):
        gathered(0, o).wait_recv()

    first_hop(0).start()
    first_hop(1).start()
    give_edges(0, x, nl, nr, 0)
    centre(x)
    own_w[0].wait()
    push_w[0].wait_recv()
    total = near_conv(qs, 64, 256, w1, True, (0,))
    take(0)
    sides(x, nl, nr)
    act, der = gelu_parts(total + near_conv(qs, 64, 256, w1, True, (-1, 1)) + b1_ref[...])
    slope[inner] = der.reshape(16, 16, C)
    h[inner] = (x[inner].reshape(256, C).astype(F32) + act).astype(BF16).reshape(16, 16, C)
    give_block(2, h, hl, hr, 3 + zhi, 15)

    for slot in (0, 1):
        first_hop(slot).wait_recv()
        second_hop(slot, False).start()
    for o in range(1, T):
        gathered(1, o).wait_recv()
    first_hop(2).start()
    first_hop(3).start()
    own_w[1].wait()
    push_w[1].wait_recv()
    second_hop(0, True).wait_recv()
    second_hop(1, True).wait_recv()
    give_far_edges(1, x, nl, nr, 0)
    for slot in (2, 3):
        first_hop(slot).wait_recv()
        second_hop(slot, False).start()

    def second_forward(start, count):
        window = pl.ds(start, count)
        _, der = gelu_parts(far_conv((hl, h, hr), start, count, w2, True) + b2_ref[...])
        a[window] = (der * ct[window].reshape(16 * count, C).astype(F32)).astype(BF16).reshape(count, 16, C)

    take(2)
    early = 3 + 2 * zhi
    second_forward(early, 14)
    give_block(4, a, al, ar, early, 14)

    take(1)
    centre_far(x)
    sides_far(x, nl, nr)
    late = 18 * (1 - zhi)
    for j in range(3):
        qf[j] = qs[j, pl.ds(pl.multiple_of(16 * late, 16), 96)]
    act, der = gelu_parts(near_conv(qf, 16, 64, w1, True, (-1, 0, 1)) + b1_ref[...])
    window = pl.ds(late, 4)
    slope[window] = der.reshape(4, 16, C)
    h[window] = (x[window].reshape(64, C).astype(F32) + act).astype(BF16).reshape(4, 16, C)
    give_block(3, h, hl, hr, late, 4)
    second_hop(2, True).wait_recv()
    second_hop(3, True).wait_recv()
    take(3)
    late = 17 - 16 * zhi
    second_forward(late, 4)
    give_block(5, a, al, ar, late, 4)

    def second_adjoint(start, count):
        window = pl.ds(start, count)
        hidden_adj = ct[window].reshape(16 * count, C).astype(F32) + far_conv((al, a, ar), start, count, w2, False)
        adj[window] = hidden_adj.reshape(count, 16, C)
        f[window] = (slope[window].reshape(16 * count, C) * hidden_adj).astype(BF16).reshape(count, 16, C)

    take(4)
    second_adjoint(3 + 3 * zhi, 13)
    take(5)
    second_adjoint(16 - 14 * zhi, 4)

    give_edges(6, f, ml, mr, 1)
    give_far_edges(7, f, ml, mr, 1)
    centre(f)
    centre_far(f)
    total = adj[inner].reshape(256, C) + near_conv(qs, 64, 256, w1, False, (0,))
    take(6)
    take(7)
    sides(f, ml, mr)
    sides_far(f, ml, mr)
    total = total + near_conv(qs, 64, 256, w1, False, (-1, 1))
    pre[...] = total.reshape(16, 2, 8, C)

    swap = remote(pre.at[:, 1 - p], psum_in, ps, pr, {"path": 1 - p})
    swap.start()
    swap.wait()
    pre[:, p] = pre[:, p] + psum_in[...]

    def collect(o):
        d = (me + o) % T
        return remote(pre.at[d, p], back.at[me], os_.at[o], or_.at[o], {"lon": zhi * T + d})

    def collected(o):
        s = (me + T - o) % T
        return remote(pre.at[s, p], back.at[s], os_.at[o], or_.at[o], {"lon": zhi * T + s})

    for o in range(1, T):
        collect(o).start()
    back[me] = pre[me, p]
    for stage, left_src, right_src, at_left, at_right in sent:
        @pl.when(has_r)
        def _():
            right_going(stage, right_src, at_left).wait_send()

        @pl.when(has_l)
        def _():
            left_going(stage, left_src, at_right).wait_send()

    for slot in range(4):
        first_hop(slot).wait_send()
        second_hop(slot, False).wait_send()
    for o in range(1, T):
        for which in (0, 1):
            spread(which, o).wait_send()
    for copy in push_w:
        copy.wait_send()
    for o in range(1, T):
        collected(o).wait_recv()
    got = back[...].reshape(128, C)
    top = got.astype(BF16)
    rest = (got - top.astype(F32)).astype(BF16)
    total = dot(join_ref[...], top) + dot(join_ref[...], rest)
    rows = pl.ds(p * 8, 8)
    diff = obs[rows].astype(F32) - base[rows].astype(F32)
    out_ref[...] = (diff * total.reshape(8, 16, C) / 2).astype(BF16)
    for o in range(1, T):
        collect(o).wait_send()


def shards(observed, baseline, cotangent, first_weight, first_bias, second_weight, second_bias):
    hbm = pl.BlockSpec(memory_space=pl.ANY)
    vmem = pl.BlockSpec(memory_space=pltpu.VMEM)
    tiles = lambda n, dtype=BF16: pltpu.VMEM((n, 16, C), dtype)
    ext = tiles(22)
    dma = pltpu.SemaphoreType.DMA
    constants = moves()
    return pl.pallas_call(
        kernel,
        out_shape=jax.ShapeDtypeStruct((8, 16, C), BF16),
        in_specs=[hbm, hbm, hbm, hbm, vmem, hbm, vmem] + [vmem] * len(constants),
        out_specs=vmem,
        scratch_shapes=[
            tiles(16), tiles(16), tiles(16), pltpu.VMEM((2, 16, 16, C), BF16),
            pltpu.VMEM((9, C, C), BF16), pltpu.VMEM((9, C, C), BF16),
            ext, ext, ext, ext, ext, ext, ext, ext, ext, tiles(6), tiles(6), tiles(6), tiles(6),
            pltpu.VMEM((2, 8, 16, C), BF16), pltpu.VMEM((2, 2, 16, C), BF16), tiles(3), tiles(2),
            pltpu.VMEM((3, 384, C), F32), pltpu.VMEM((3, 96, C), F32),
            tiles(22, F32), tiles(22, F32),
            pltpu.VMEM((16, 2, 8, C), F32), pltpu.VMEM((16, 8, C), F32), pltpu.VMEM((16, 8, C), F32),
            dma((5,)), dma((2,)), dma((2,)), dma((2, T)), dma((2, T)), dma((8, 2)), dma((8, 2)), dma((8,)), dma((8,)),
            dma, dma, dma((T,)), dma((T,)),
        ],
        compiler_params=pltpu.CompilerParams(collective_id=0, has_side_effects=True),
    )(observed, baseline, cotangent, first_weight, first_bias.reshape(1, C), second_weight,
      second_bias.reshape(1, C), *constants)


def solution(mesh):
    placed = (
        P("lon", "lat", None),
        P("lon", "lat", None),
        P("lon", "lat", None),
        P(None, "path", None),
        P(),
        P(None, "path", None),
        P(),
    )
    return jax.shard_map(
        shards,
        mesh=mesh,
        in_specs=placed,
        out_specs=P(("lon", "path"), "lat", None),
        check_vma=False,
    )
```

```python
import functools

import jax
import jax.numpy as jnp
import numpy as np
from jax import lax
from jax.experimental import pallas as pl
from jax.experimental.pallas import tpu as pltpu
from jax.sharding import PartitionSpec as P

MESH = pl.DeviceIdType.MESH
F32 = jnp.float32
BF16 = jnp.bfloat16
C = 384
T = 16


def one_hot(rows, cols, pairs):
    out = np.zeros((rows, cols), np.float32)
    for r, c in pairs:
        out[r, c] = 1.0
    return out


def moves():
    split = one_hot(256, 256, [
        ((4 * s + c) * 16 + 4 * k + q, (4 * k + c) * 16 + 4 * q + s)
        for s in range(4) for c in range(4) for k in range(4) for q in range(4)])
    edges = one_hot(128, 256, [(m, 4 * m) for m in range(64)] + [(64 + m, 4 * m + 3) for m in range(64)])
    edges_far = one_hot(32, 48, [(m, 4 * m) for m in range(12)] + [(16 + m, 4 * m + 3) for m in range(12)])

    def shift(rows, total, step):
        edge = 0 if step < 0 else 3
        return one_hot(4 * rows, total, [
            (4 * m + q, 4 * rows + m if q == edge else 4 * m + q + step) for m in range(rows) for q in range(4)])

    join = one_hot(128, 128, [
        ((4 * k + c) * 16 + 4 * q + s, (4 * s + c) * 8 + 4 * k + q)
        for s in range(4) for c in range(4) for k in range(2) for q in range(4)])
    parts = (split, edges, edges_far, shift(64, 320, -1), shift(64, 320, 1), shift(12, 64, -1), shift(12, 64, 1), join)
    return jnp.asarray(np.concatenate([np.pad(v, ((0, 0), (0, 384 - v.shape[1]))) for v in parts]), BF16)


def dot(a, b):
    return lax.dot_general(a, b, (((1,), (0,)), ((), ())), preferred_element_type=F32)


def dot_t(a, b):
    return lax.dot_general(a, b, (((1,), (1,)), ((), ())), preferred_element_type=F32)


ROOT = 0.7978845608028654


def gelu_parts(x):
    square = x * x
    t = jnp.tanh(ROOT * (x + 0.044715 * (x * square)))
    half = 0.5 * (1.0 + t)
    slope = half + 0.5 * x * (1.0 - t * t) * (ROOT * (1.0 + 3 * 0.044715 * square))
    return x * half, slope


def kernel(obs_h, base_h, cot_h, w1_h, b1_h, w2_h, b2_h, moves_h,
           out_ref,
           table, b1_ref, b2_ref, obs, base, cot, snd, w1, w2, x, ct, h, hl, hr, a, al, ar, f, nl, nr, ml, mr, pk, pkf,
           qs, qf, slope, adj, pre, psum_in, back,
           ls, ws, wr, as_, ar_, es, er, fs, fr, ps, pr, os_, or_):
    p = lax.axis_index("path")
    lon = lax.axis_index("lon")
    lat = lax.axis_index("lat")
    me = lon % T
    zhi = lon // T
    has_l = lat > 0
    has_r = lat < 7

    across = {"lon": (lon + T) % (2 * T)}

    loads = [pltpu.make_async_copy(src, dst, ls.at[i]) for i, (src, dst) in enumerate(
        ((obs_h, obs), (base_h, base), (cot_h, cot)))]
    half = pl.ds(pl.multiple_of(p * 192, 64), 192)
    own_w = [pltpu.make_async_copy(src, dst.at[:, half, :], ls.at[3 + i]) for i, (src, dst) in enumerate(
        ((w1_h, w1), (w2_h, w2)))]
    more = [pltpu.make_async_copy(src, dst, ls.at[5 + i]) for i, (src, dst) in enumerate(
        ((moves_h, table), (b1_h, b1_ref), (b2_h, b2_ref)))]

    barrier = pltpu.get_barrier_semaphore()

    def greet(**where):
        pl.semaphore_signal(barrier, inc=1, device_id=where, device_id_type=MESH)

    for o in range(1, T):
        greet(lon=zhi * T + (me + o) % T)
    greet(path=1 - p)
    greet(**across)

    @pl.when(has_l)
    def _():
        greet(lat=lat - 1)

    @pl.when(has_r)
    def _():
        greet(lat=lat + 1)

    for copy in loads + more + own_w:
        copy.start()

    starts = np.cumsum([0, 256, 128, 32, 256, 256, 48, 48])
    split_ref, edges_ref, edges_far_ref, minus_ref, plus_ref, minus_far_ref, plus_far_ref, join_ref = (
        table.at[int(first):int(first) + size, :width] for first, size, width in zip(
            starts, (256, 128, 32, 256, 256, 48, 48, 128), (256, 256, 48, 384, 384, 128, 128, 128)))

    outside = 2 + 17 * zhi
    past = 19 * (1 - zhi)
    blank = jnp.zeros((16, C), BF16)
    for ref in (h, hl, hr, a, al, ar):
        ref[outside] = blank
    for ref in (nl, nr, ml, mr):
        ref[0] = blank
        ref[5] = blank
    for t in (0, 1, 2, 19, 20, 21):
        f[t] = blank
    for j in range(3):
        qs[j, :64] = jnp.zeros((64, C), F32)
        qs[j, 320:] = jnp.zeros((64, C), F32)

    @pl.when(jnp.logical_not(has_l))
    def _():
        for ref in (hl, al, nl, ml):
            ref[...] = jnp.zeros(ref.shape, BF16)

    @pl.when(jnp.logical_not(has_r))
    def _():
        for ref in (hr, ar, nr, mr):
            ref[...] = jnp.zeros(ref.shape, BF16)

    for copy in loads + more:
        copy.wait()
    low = base[...].astype(F32)
    mix = (p.astype(F32) + 0.5) / 2
    field = (low + mix * (obs[...].astype(F32) - low)).astype(BF16)
    snd[0] = dot(split_ref[...], field.reshape(256, C)).astype(BF16).reshape(T, 16, C)
    snd[1] = dot(split_ref[...], cot[...].reshape(256, C)).astype(BF16).reshape(T, 16, C)

    pl.semaphore_wait(barrier, 17 + has_l.astype(jnp.int32) + has_r.astype(jnp.int32))

    def remote(src, dst, send_sem, recv_sem, where):
        return pltpu.make_async_remote_copy(
            src_ref=src, dst_ref=dst, send_sem=send_sem, recv_sem=recv_sem, device_id=where, device_id_type=MESH)

    def spread(which, o):
        d = (me + o) % T
        dst = (x, ct)[which].at[3 + me]
        return remote(snd.at[which, d], dst, as_.at[which, o], ar_.at[which, o], {"lon": zhi * T + d})

    def gathered(which, o):
        s = (me + T - o) % T
        dst = (x, ct)[which].at[3 + s]
        return remote(snd.at[which, s], dst, as_.at[which, o], ar_.at[which, o], {"lon": zhi * T + s})

    for o in range(1, T):
        spread(0, o).start()
    push_w = [remote(src, dst.at[:, half, :], ws.at[i], wr.at[i], {"path": 1 - p})
              for i, (src, dst) in enumerate(((w1_h, w1), (w2_h, w2)))]
    push_w[0].start()
    for o in range(1, T):
        spread(1, o).start()
    push_w[1].start()
    x[3 + me] = snd[0, me]
    ct[3 + me] = snd[1, me]

    def seam(slot, coming=False):
        side = 1 - zhi if coming else zhi
        ref, base, at, count = ((x, 16 - 13 * zhi, 19 * side, 3), (ct, 17 - 14 * zhi, 1 + 18 * side, 2))[slot]
        return remote(ref.at[pl.ds(base, count)], ref.at[pl.ds(at, count)], fs.at[slot], fr.at[slot], across)

    def right_going(stage, src, dst):
        return remote(src, dst, es.at[stage, 0], er.at[stage, 0], {"lat": lat + 1})

    def left_going(stage, src, dst):
        return remote(src, dst, es.at[stage, 1], er.at[stage, 1], {"lat": lat - 1})

    sent = []

    def give(stage, left_src, right_src, at_left, at_right):
        @pl.when(has_r)
        def _():
            right_going(stage, right_src, at_left).start()

        @pl.when(has_l)
        def _():
            left_going(stage, left_src, at_right).start()

        sent.append((stage, left_src, right_src, at_left, at_right))

    def take(stage):
        left_src, right_src, at_left, at_right = next(v[1:] for v in sent if v[0] == stage)

        @pl.when(has_l)
        def _():
            right_going(stage, right_src, at_left).wait_recv()

        @pl.when(has_r)
        def _():
            left_going(stage, left_src, at_right).wait_recv()

    def give_block(stage, main, left, right, start, count):
        window = pl.ds(start, count)
        give(stage, main.at[window], main.at[window], left.at[window], right.at[window])

    inner = pl.ds(3, 16)
    beyond = pl.ds(past, 3)
    edge = 5 * (1 - zhi)

    def give_edges(stage, main, left, right, layer):
        pk[layer] = dot(edges_ref[...], main[inner].reshape(256, C)).astype(BF16).reshape(8, 16, C)
        give(stage, pk.at[layer, pl.ds(0, 4)], pk.at[layer, pl.ds(4, 4)], left.at[pl.ds(1, 4)], right.at[pl.ds(1, 4)])

    def give_far_edges(stage, main, left, right, layer):
        pkf[layer] = dot(edges_far_ref[...], main[beyond].reshape(48, C)).astype(BF16).reshape(2, 16, C)
        give(stage, pkf.at[layer, pl.ds(0, 1)], pkf.at[layer, pl.ds(1, 1)],
             left.at[pl.ds(edge, 1)], right.at[pl.ds(edge, 1)])

    far_rows = pl.ds(pl.multiple_of(16 * (1 + past), 16), 48)

    def centre(main):
        qs[1, 64:320] = main[inner].reshape(256, C).astype(F32)

    def centre_far(main):
        qs[1, far_rows] = main[beyond].reshape(48, C).astype(F32)

    def sides(main, left, right):
        whole = main[inner].reshape(256, C)
        for j, move, outer in ((0, minus_ref, left), (2, plus_ref, right)):
            qs[j, 64:320] = dot(move[:, :256], whole) + dot(move[:, 256:320], outer[pl.ds(1, 4)].reshape(64, C))

    def sides_far(main, left, right):
        whole = main[beyond].reshape(48, C)
        for j, move, outer in ((0, minus_far_ref, left), (2, plus_far_ref, right)):
            qs[j, far_rows] = dot(move[:, :48], whole) + dot(move[:, 48:64], outer[edge])

    def near_conv(ref, first, rows, weights, forward, columns):
        total = jnp.zeros((rows, C), F32)
        sign = 1 if forward else -1
        for j in columns:
            for i in (-1, 0, 1):
                window = ref[1 + sign * j, pl.ds(first + 4 * sign * i, rows), :].astype(BF16)
                total = total + (dot if forward else dot_t)(window, weights[3 * (i + 1) + j + 1])
        return total

    def far_conv(parts, start, count, weights, forward):
        total = jnp.zeros((16 * count, C), F32)
        sign = 1 if forward else -1
        for j in (0, -1, 1):
            for i in (-1, 0, 1):
                window = parts[1 + sign * j][pl.ds(start + sign * i, count)].reshape(16 * count, C)
                total = total + (dot if forward else dot_t)(window, weights[3 * (i + 1) + j + 1])
        return total

    for o in range(1, T):
        gathered(0, o).wait_recv()

    seam(0).start()
    give_edges(0, x, nl, nr, 0)
    centre(x)
    own_w[0].wait()
    push_w[0].wait_recv()
    total = near_conv(qs, 64, 256, w1, True, (0,))
    take(0)
    sides(x, nl, nr)
    act, der = gelu_parts(total + near_conv(qs, 64, 256, w1, True, (-1, 1)) + b1_ref[...])
    slope[inner] = der.reshape(16, 16, C)
    h[inner] = (x[inner].reshape(256, C).astype(F32) + act).astype(BF16).reshape(16, 16, C)
    give_block(2, h, hl, hr, 3 + zhi, 15)

    for o in range(1, T):
        gathered(1, o).wait_recv()
    seam(1).start()
    own_w[1].wait()
    push_w[1].wait_recv()
    seam(0, True).wait_recv()
    give_far_edges(1, x, nl, nr, 0)

    def second_forward(start, count):
        window = pl.ds(start, count)
        _, der = gelu_parts(far_conv((hl, h, hr), start, count, w2, True) + b2_ref[...])
        a[window] = (der * ct[window].reshape(16 * count, C).astype(F32)).astype(BF16).reshape(count, 16, C)

    take(2)
    early = 3 + 2 * zhi
    second_forward(early, 14)
    give_block(4, a, al, ar, early, 14)

    take(1)
    centre_far(x)
    sides_far(x, nl, nr)
    late = 18 * (1 - zhi)
    for j in range(3):
        qf[j] = qs[j, pl.ds(pl.multiple_of(16 * late, 16), 96)]
    act, der = gelu_parts(near_conv(qf, 16, 64, w1, True, (-1, 0, 1)) + b1_ref[...])
    window = pl.ds(late, 4)
    slope[window] = der.reshape(4, 16, C)
    h[window] = (x[window].reshape(64, C).astype(F32) + act).astype(BF16).reshape(4, 16, C)
    give_block(3, h, hl, hr, late, 4)
    seam(1, True).wait_recv()
    take(3)
    late = 17 - 16 * zhi
    second_forward(late, 4)
    give_block(5, a, al, ar, late, 4)

    def second_adjoint(start, count):
        window = pl.ds(start, count)
        hidden_adj = ct[window].reshape(16 * count, C).astype(F32) + far_conv((al, a, ar), start, count, w2, False)
        adj[window] = hidden_adj.reshape(count, 16, C)
        f[window] = (slope[window].reshape(16 * count, C) * hidden_adj).astype(BF16).reshape(count, 16, C)

    take(4)
    second_adjoint(3 + 3 * zhi, 13)
    take(5)
    second_adjoint(16 - 14 * zhi, 4)

    give_edges(6, f, ml, mr, 1)
    give_far_edges(7, f, ml, mr, 1)
    centre(f)
    centre_far(f)
    total = adj[inner].reshape(256, C) + near_conv(qs, 64, 256, w1, False, (0,))
    take(6)
    take(7)
    sides(f, ml, mr)
    sides_far(f, ml, mr)
    pre[...] = total.reshape(16, 2, 8, C)

    def swap(part):
        tiles = pl.ds(8 * part, 8)
        return remote(pre.at[tiles, 1 - p], psum_in.at[tiles], ps.at[part], pr.at[part], {"path": 1 - p})

    def collect(d):
        return remote(pre.at[d, p], back.at[me], os_.at[d], or_.at[me], {"lon": zhi * T + d})

    def collected(s):
        return remote(pre.at[s, p], back.at[s], os_.at[s], or_.at[s], {"lon": zhi * T + s})

    for part in (0, 1):
        rest = near_conv(qs, 64 + 128 * part, 128, w1, False, (-1, 1))
        tiles = pl.ds(8 * part, 8)
        pre[tiles] = pre[tiles] + rest.reshape(8, 2, 8, C)
        swap(part).start()
    for part in (0, 1):
        swap(part).wait()
        tiles = pl.ds(8 * part, 8)
        pre[tiles, p] = pre[tiles, p] + psum_in[tiles]
        for d in range(8 * part, 8 * part + 8):
            @pl.when(me != d)
            def _():
                collect(d).start()
    back[me] = pre[me, p]
    for stage, left_src, right_src, at_left, at_right in sent:
        @pl.when(has_r)
        def _():
            right_going(stage, right_src, at_left).wait_send()

        @pl.when(has_l)
        def _():
            left_going(stage, left_src, at_right).wait_send()

    seam(0).wait_send()
    seam(1).wait_send()
    for o in range(1, T):
        for which in (0, 1):
            spread(which, o).wait_send()
    for copy in push_w:
        copy.wait_send()
    for o in range(1, T):
        collected((me + o) % T).wait_recv()
    got = back[...].reshape(128, C)
    top = got.astype(BF16)
    rest = (got - top.astype(F32)).astype(BF16)
    total = dot(join_ref[...], top) + dot(join_ref[...], rest)
    rows = pl.ds(p * 8, 8)
    diff = obs[rows].astype(F32) - base[rows].astype(F32)
    out_ref[...] = (diff * total.reshape(8, 16, C) / 2).astype(BF16)
    for o in range(1, T):
        collect((me + o) % T).wait_send()


def shards(observed, baseline, cotangent, first_weight, first_bias, second_weight, second_bias):
    hbm = pl.BlockSpec(memory_space=pl.ANY)
    vmem = pl.BlockSpec(memory_space=pltpu.VMEM)
    tiles = lambda n, dtype=BF16: pltpu.VMEM((n, 16, C), dtype)
    ext = tiles(22)
    dma = pltpu.SemaphoreType.DMA
    constants = moves()
    return pl.pallas_call(
        kernel,
        out_shape=jax.ShapeDtypeStruct((8, 16, C), BF16),
        in_specs=[hbm] * 8,
        out_specs=vmem,
        scratch_shapes=[
            pltpu.VMEM(constants.shape, BF16), pltpu.VMEM((1, C), F32), pltpu.VMEM((1, C), F32),
            tiles(16), tiles(16), tiles(16), pltpu.VMEM((2, 16, 16, C), BF16),
            pltpu.VMEM((9, C, C), BF16), pltpu.VMEM((9, C, C), BF16),
            ext, ext, ext, ext, ext, ext, ext, ext, ext, tiles(6), tiles(6), tiles(6), tiles(6),
            pltpu.VMEM((2, 8, 16, C), BF16), pltpu.VMEM((2, 2, 16, C), BF16),
            pltpu.VMEM((3, 384, C), F32), pltpu.VMEM((3, 96, C), F32),
            tiles(22, F32), tiles(22, F32),
            pltpu.VMEM((16, 2, 8, C), F32), pltpu.VMEM((16, 8, C), F32), pltpu.VMEM((16, 8, C), F32),
            dma((8,)), dma((2,)), dma((2,)), dma((2, T)), dma((2, T)), dma((8, 2)), dma((8, 2)), dma((2,)), dma((2,)),
            dma((2,)), dma((2,)), dma((T,)), dma((T,)),
        ],
        compiler_params=pltpu.CompilerParams(collective_id=0, has_side_effects=True),
    )(observed, baseline, cotangent, first_weight, first_bias.reshape(1, C), second_weight,
      second_bias.reshape(1, C), constants)


def solution(mesh):
    placed = (
        P("lon", "lat", None),
        P("lon", "lat", None),
        P("lon", "lat", None),
        P(None, "path", None),
        P(),
        P(None, "path", None),
        P(),
    )
    return jax.shard_map(
        shards,
        mesh=mesh,
        in_specs=placed,
        out_specs=P(("lon", "path"), "lat", None),
        check_vma=False,
    )
```

```python
import functools

import jax
import jax.numpy as jnp
import numpy as np
from jax import lax
from jax.experimental import pallas as pl
from jax.experimental.pallas import tpu as pltpu
from jax.sharding import PartitionSpec as P

MESH = pl.DeviceIdType.MESH
F32 = jnp.float32
BF16 = jnp.bfloat16
C = 384
T = 16


def one_hot(rows, cols, pairs):
    out = np.zeros((rows, cols), np.float32)
    for r, c in pairs:
        out[r, c] = 1.0
    return out


def moves():
    split = one_hot(256, 256, [
        ((4 * s + c) * 16 + 4 * k + q, (4 * k + c) * 16 + 4 * q + s)
        for s in range(4) for c in range(4) for k in range(4) for q in range(4)])
    edges = one_hot(128, 256, [(m, 4 * m) for m in range(64)] + [(64 + m, 4 * m + 3) for m in range(64)])
    edges_far = one_hot(32, 48, [(m, 4 * m) for m in range(12)] + [(16 + m, 4 * m + 3) for m in range(12)])

    def shift(rows, total, step):
        edge = 0 if step < 0 else 3
        return one_hot(4 * rows, total, [
            (4 * m + q, 4 * rows + m if q == edge else 4 * m + q + step) for m in range(rows) for q in range(4)])

    join = one_hot(128, 128, [
        ((4 * k + c) * 16 + 4 * q + s, (4 * s + c) * 8 + 4 * k + q)
        for s in range(4) for c in range(4) for k in range(2) for q in range(4)])
    parts = (split, edges, edges_far, shift(64, 320, -1), shift(64, 320, 1), shift(12, 64, -1), shift(12, 64, 1), join)
    return jnp.asarray(np.concatenate([np.pad(v, ((0, 0), (0, 384 - v.shape[1]))) for v in parts]), BF16)


def dot(a, b):
    return lax.dot_general(a, b, (((1,), (0,)), ((), ())), preferred_element_type=F32)


def dot_t(a, b):
    return lax.dot_general(a, b, (((1,), (1,)), ((), ())), preferred_element_type=F32)


ROOT = 0.7978845608028654


def gelu_parts(x):
    square = x * x
    t = jnp.tanh(ROOT * (x + 0.044715 * (x * square)))
    half = 0.5 * (1.0 + t)
    slope = half + 0.5 * x * (1.0 - t * t) * (ROOT * (1.0 + 3 * 0.044715 * square))
    return x * half, slope


def kernel(obs_h, base_h, cot_h, w1_h, b1_h, w2_h, b2_h, moves_h,
           out_ref,
           table, b1_ref, b2_ref, obs, base, cot, snd, w1, w2, x, ct, h, hl, hr, a, al, ar, f, nl, nr, ml, mr, pk, pkf,
           qs, qf, slope, adj, pre, back,
           ls, ws, wr, as_, ar_, es, er, fs, fr, os_, or_, near_up, near_down, mid_up, mid_down, wide_up, wide_down):
    p = lax.axis_index("path")
    lon = lax.axis_index("lon")
    lat = lax.axis_index("lat")
    me = lon % T
    zhi = lon // T
    has_l = lat > 0
    has_r = lat < 7

    z = zhi * 8 + lat
    across = {"lon": (lon + T) % (2 * T)}

    def along(step):
        there = (z + step + 16) % 16
        return {"lon": (there // 8) * T + me, "lat": there % 8}

    loads = [pltpu.make_async_copy(src, dst, ls.at[i]) for i, (src, dst) in enumerate(
        ((obs_h, obs), (base_h, base), (cot_h, cot)))]
    half = pl.ds(pl.multiple_of(p * 192, 64), 192)
    own_w = [pltpu.make_async_copy(src, dst.at[:, half, :], ls.at[3 + i]) for i, (src, dst) in enumerate(
        ((w1_h, w1), (w2_h, w2)))]
    more = [pltpu.make_async_copy(src, dst, ls.at[5 + i]) for i, (src, dst) in enumerate(
        ((moves_h, table), (b1_h, b1_ref), (b2_h, b2_ref)))]

    barrier = pltpu.get_barrier_semaphore()

    def greet(**where):
        pl.semaphore_signal(barrier, inc=1, device_id=where, device_id_type=MESH)

    for o in range(1, T):
        greet(lon=zhi * T + (me + o) % T)
    greet(path=1 - p)
    greet(**along(1))
    greet(**along(-1))

    for copy in loads + more + own_w:
        copy.start()

    starts = np.cumsum([0, 256, 128, 32, 256, 256, 48, 48])
    split_ref, edges_ref, edges_far_ref, minus_ref, plus_ref, minus_far_ref, plus_far_ref, join_ref = (
        table.at[int(first):int(first) + size, :width] for first, size, width in zip(
            starts, (256, 128, 32, 256, 256, 48, 48, 128), (256, 256, 48, 384, 384, 128, 128, 128)))

    outside = 2 + 17 * zhi
    past = 19 * (1 - zhi)
    blank = jnp.zeros((16, C), BF16)
    for ref in (h, hl, hr, a, al, ar):
        ref[outside] = blank
    for ref in (nl, nr, ml, mr):
        ref[0] = blank
        ref[5] = blank
    for t in (0, 1, 2, 19, 20, 21):
        f[t] = blank
    for j in range(3):
        qs[j, :64] = jnp.zeros((64, C), F32)
        qs[j, 320:] = jnp.zeros((64, C), F32)

    @pl.when(jnp.logical_not(has_l))
    def _():
        for ref in (hl, al, nl, ml):
            ref[...] = jnp.zeros(ref.shape, BF16)

    @pl.when(jnp.logical_not(has_r))
    def _():
        for ref in (hr, ar, nr, mr):
            ref[...] = jnp.zeros(ref.shape, BF16)

    for copy in loads + more:
        copy.wait()
    low = base[...].astype(F32)
    mix = (p.astype(F32) + 0.5) / 2
    field = (low + mix * (obs[...].astype(F32) - low)).astype(BF16)
    snd[0] = dot(split_ref[...], field.reshape(256, C)).astype(BF16).reshape(T, 16, C)
    snd[1] = dot(split_ref[...], cot[...].reshape(256, C)).astype(BF16).reshape(T, 16, C)

    pl.semaphore_wait(barrier, 18)

    def remote(src, dst, send_sem, recv_sem, where):
        return pltpu.make_async_remote_copy(
            src_ref=src, dst_ref=dst, send_sem=send_sem, recv_sem=recv_sem, device_id=where, device_id_type=MESH)

    def spread(which, o):
        d = (me + o) % T
        dst = (x, ct)[which].at[3 + me]
        return remote(snd.at[which, d], dst, as_.at[which, o], ar_.at[which, o], {"lon": zhi * T + d})

    def gathered(which, o):
        s = (me + T - o) % T
        dst = (x, ct)[which].at[3 + s]
        return remote(snd.at[which, s], dst, as_.at[which, o], ar_.at[which, o], {"lon": zhi * T + s})

    for o in range(1, T):
        spread(0, o).start()
    push_w = [remote(src, dst.at[:, half, :], ws.at[i], wr.at[i], {"path": 1 - p})
              for i, (src, dst) in enumerate(((w1_h, w1), (w2_h, w2)))]
    push_w[0].start()
    for o in range(1, T):
        spread(1, o).start()
    push_w[1].start()
    x[3 + me] = snd[0, me]
    ct[3 + me] = snd[1, me]

    for step, up, down in ((1, near_up, near_down), (2, mid_up, mid_down), (4, wide_up, wide_down)):
        pl.semaphore_signal(up, inc=1, device_id=along(step), device_id_type=MESH)
        pl.semaphore_signal(down, inc=1, device_id=along(-step), device_id_type=MESH)
        pl.semaphore_wait(up, 1)
        pl.semaphore_wait(down, 1)

    def seam(slot, coming=False):
        side = 1 - zhi if coming else zhi
        ref, base, at, count = ((x, 16 - 13 * zhi, 19 * side, 3), (ct, 17 - 14 * zhi, 1 + 18 * side, 2))[slot]
        return remote(ref.at[pl.ds(base, count)], ref.at[pl.ds(at, count)], fs.at[slot], fr.at[slot], across)

    def right_going(stage, src, dst):
        return remote(src, dst, es.at[stage, 0], er.at[stage, 0], {"lat": lat + 1})

    def left_going(stage, src, dst):
        return remote(src, dst, es.at[stage, 1], er.at[stage, 1], {"lat": lat - 1})

    sent = []

    def give(stage, left_src, right_src, at_left, at_right):
        @pl.when(has_r)
        def _():
            right_going(stage, right_src, at_left).start()

        @pl.when(has_l)
        def _():
            left_going(stage, left_src, at_right).start()

        sent.append((stage, left_src, right_src, at_left, at_right))

    def take(stage):
        left_src, right_src, at_left, at_right = next(v[1:] for v in sent if v[0] == stage)

        @pl.when(has_l)
        def _():
            right_going(stage, right_src, at_left).wait_recv()

        @pl.when(has_r)
        def _():
            left_going(stage, left_src, at_right).wait_recv()

    def give_block(stage, main, left, right, start, count):
        window = pl.ds(start, count)
        give(stage, main.at[window], main.at[window], left.at[window], right.at[window])

    inner = pl.ds(3, 16)
    beyond = pl.ds(past, 3)
    edge = 5 * (1 - zhi)

    def give_edges(stage, main, left, right, layer):
        pk[layer] = dot(edges_ref[...], main[inner].reshape(256, C)).astype(BF16).reshape(8, 16, C)
        give(stage, pk.at[layer, pl.ds(0, 4)], pk.at[layer, pl.ds(4, 4)], left.at[pl.ds(1, 4)], right.at[pl.ds(1, 4)])

    def give_far_edges(stage, main, left, right, layer):
        pkf[layer] = dot(edges_far_ref[...], main[beyond].reshape(48, C)).astype(BF16).reshape(2, 16, C)
        give(stage, pkf.at[layer, pl.ds(0, 1)], pkf.at[layer, pl.ds(1, 1)],
             left.at[pl.ds(edge, 1)], right.at[pl.ds(edge, 1)])

    far_rows = pl.ds(pl.multiple_of(16 * (1 + past), 16), 48)

    def centre(main):
        qs[1, 64:320] = main[inner].reshape(256, C).astype(F32)

    def centre_far(main):
        qs[1, far_rows] = main[beyond].reshape(48, C).astype(F32)

    def sides(main, left, right):
        whole = main[inner].reshape(256, C)
        for j, move, outer in ((0, minus_ref, left), (2, plus_ref, right)):
            qs[j, 64:320] = dot(move[:, :256], whole) + dot(move[:, 256:320], outer[pl.ds(1, 4)].reshape(64, C))

    def sides_far(main, left, right):
        whole = main[beyond].reshape(48, C)
        for j, move, outer in ((0, minus_far_ref, left), (2, plus_far_ref, right)):
            qs[j, far_rows] = dot(move[:, :48], whole) + dot(move[:, 48:64], outer[edge])

    def near_conv(ref, first, rows, weights, forward, columns):
        total = jnp.zeros((rows, C), F32)
        sign = 1 if forward else -1
        for j in columns:
            for i in (-1, 0, 1):
                window = ref[1 + sign * j, pl.ds(first + 4 * sign * i, rows), :].astype(BF16)
                total = total + (dot if forward else dot_t)(window, weights[3 * (i + 1) + j + 1])
        return total

    def far_conv(parts, start, count, weights, forward):
        total = jnp.zeros((16 * count, C), F32)
        sign = 1 if forward else -1
        for j in (0, -1, 1):
            for i in (-1, 0, 1):
                window = parts[1 + sign * j][pl.ds(start + sign * i, count)].reshape(16 * count, C)
                total = total + (dot if forward else dot_t)(window, weights[3 * (i + 1) + j + 1])
        return total

    for o in range(1, T):
        gathered(0, o).wait_recv()

    seam(0).start()
    give_edges(0, x, nl, nr, 0)
    centre(x)
    own_w[0].wait()
    push_w[0].wait_recv()
    total = near_conv(qs, 64, 256, w1, True, (0,))
    take(0)
    sides(x, nl, nr)
    act, der = gelu_parts(total + near_conv(qs, 64, 256, w1, True, (-1, 1)) + b1_ref[...])
    slope[inner] = der.reshape(16, 16, C)
    h[inner] = (x[inner].reshape(256, C).astype(F32) + act).astype(BF16).reshape(16, 16, C)
    give_block(2, h, hl, hr, 3 + 8 * zhi, 8)
    give_block(8, h, hl, hr, 11 - 7 * zhi, 7)

    for o in range(1, T):
        gathered(1, o).wait_recv()
    seam(1).start()
    own_w[1].wait()
    push_w[1].wait_recv()
    seam(0, True).wait_recv()
    give_far_edges(1, x, nl, nr, 0)

    def second_forward(start, count):
        window = pl.ds(start, count)
        _, der = gelu_parts(far_conv((hl, h, hr), start, count, w2, True) + b2_ref[...])
        a[window] = (der * ct[window].reshape(16 * count, C).astype(F32)).astype(BF16).reshape(count, 16, C)

    take(2)
    early = 3 + 9 * zhi
    second_forward(early, 7)
    give_block(4, a, al, ar, early, 7)
    take(8)
    early = 10 - 5 * zhi
    second_forward(early, 7)
    give_block(9, a, al, ar, early, 7)

    take(1)
    centre_far(x)
    sides_far(x, nl, nr)
    late = 18 * (1 - zhi)
    for j in range(3):
        qf[j] = qs[j, pl.ds(pl.multiple_of(16 * late, 16), 96)]
    act, der = gelu_parts(near_conv(qf, 16, 64, w1, True, (-1, 0, 1)) + b1_ref[...])
    window = pl.ds(late, 4)
    slope[window] = der.reshape(4, 16, C)
    h[window] = (x[window].reshape(64, C).astype(F32) + act).astype(BF16).reshape(4, 16, C)
    give_block(3, h, hl, hr, late, 4)
    seam(1, True).wait_recv()
    take(3)
    late = 17 - 16 * zhi
    second_forward(late, 4)
    give_block(5, a, al, ar, late, 4)

    def second_adjoint(start, count):
        window = pl.ds(start, count)
        hidden_adj = ct[window].reshape(16 * count, C).astype(F32) + far_conv((al, a, ar), start, count, w2, False)
        adj[window] = hidden_adj.reshape(count, 16, C)
        f[window] = (slope[window].reshape(16 * count, C) * hidden_adj).astype(BF16).reshape(count, 16, C)

    take(4)
    second_adjoint(3 + 10 * zhi, 6)
    take(9)
    second_adjoint(9 - 3 * zhi, 7)
    take(5)
    second_adjoint(16 - 14 * zhi, 4)

    give_edges(6, f, ml, mr, 1)
    give_far_edges(7, f, ml, mr, 1)
    centre(f)
    centre_far(f)
    total = adj[inner].reshape(256, C) + near_conv(qs, 64, 256, w1, False, (0,))
    take(6)
    take(7)
    sides(f, ml, mr)
    sides_far(f, ml, mr)
    total = total + near_conv(qs, 64, 256, w1, False, (-1, 1))
    pre[...] = total.reshape(16, 2, 8, C).astype(BF16)

    def collect(o, core):
        d = (me + o) % T
        return remote(pre.at[d, core], back.at[p, me], os_.at[o, core], or_.at[o, p],
                      {"lon": zhi * T + d, "path": core})

    def collected(o, core):
        s = (me + T - o) % T
        return remote(pre.at[s, p], back.at[core, s], os_.at[o, core], or_.at[o, core],
                      {"lon": zhi * T + s, "path": core})

    for o in range(T):
        for core in (p, 1 - p)[0 if o else 1:]:
            collect(o, core).start()
    back[p, me] = pre[me, p]
    for stage, left_src, right_src, at_left, at_right in sent:
        @pl.when(has_r)
        def _():
            right_going(stage, right_src, at_left).wait_send()

        @pl.when(has_l)
        def _():
            left_going(stage, left_src, at_right).wait_send()

    seam(0).wait_send()
    seam(1).wait_send()
    for o in range(1, T):
        for which in (0, 1):
            spread(which, o).wait_send()
    for copy in push_w:
        copy.wait_send()
    for o in range(T):
        for core in (p, 1 - p)[0 if o else 1:]:
            collected(o, core).wait_recv()
    total = dot(join_ref[...], back[0].reshape(128, C)) + dot(join_ref[...], back[1].reshape(128, C))
    rows = pl.ds(p * 8, 8)
    diff = obs[rows].astype(F32) - base[rows].astype(F32)
    out_ref[...] = (diff * total.reshape(8, 16, C) / 2).astype(BF16)
    for o in range(T):
        for core in (p, 1 - p)[0 if o else 1:]:
            collect(o, core).wait_send()


def shards(observed, baseline, cotangent, first_weight, first_bias, second_weight, second_bias):
    hbm = pl.BlockSpec(memory_space=pl.ANY)
    vmem = pl.BlockSpec(memory_space=pltpu.VMEM)
    tiles = lambda n, dtype=BF16: pltpu.VMEM((n, 16, C), dtype)
    ext = tiles(22)
    dma = pltpu.SemaphoreType.DMA
    constants = moves()
    return pl.pallas_call(
        kernel,
        out_shape=jax.ShapeDtypeStruct((8, 16, C), BF16),
        in_specs=[hbm] * 8,
        out_specs=vmem,
        scratch_shapes=[
            pltpu.VMEM(constants.shape, BF16), pltpu.VMEM((1, C), F32), pltpu.VMEM((1, C), F32),
            tiles(16), tiles(16), tiles(16), pltpu.VMEM((2, 16, 16, C), BF16),
            pltpu.VMEM((9, C, C), BF16), pltpu.VMEM((9, C, C), BF16),
            ext, ext, ext, ext, ext, ext, ext, ext, ext, tiles(6), tiles(6), tiles(6), tiles(6),
            pltpu.VMEM((2, 8, 16, C), BF16), pltpu.VMEM((2, 2, 16, C), BF16),
            pltpu.VMEM((3, 384, C), F32), pltpu.VMEM((3, 96, C), F32),
            tiles(22, F32), tiles(22, F32),
            pltpu.VMEM((16, 2, 8, C), BF16), pltpu.VMEM((2, 16, 8, C), BF16),
            dma((8,)), dma((2,)), dma((2,)), dma((2, T)), dma((2, T)), dma((10, 2)), dma((10, 2)), dma((2,)), dma((2,)),
            dma((T, 2)), dma((T, 2)), *[pltpu.SemaphoreType.REGULAR] * 6,
        ],
        compiler_params=pltpu.CompilerParams(collective_id=0, has_side_effects=True),
    )(observed, baseline, cotangent, first_weight, first_bias.reshape(1, C), second_weight,
      second_bias.reshape(1, C), constants)


def solution(mesh):
    placed = (
        P("lon", "lat", None),
        P("lon", "lat", None),
        P("lon", "lat", None),
        P(None, "path", None),
        P(),
        P(None, "path", None),
        P(),
    )
    return jax.shard_map(
        shards,
        mesh=mesh,
        in_specs=placed,
        out_specs=P(("lon", "path"), "lat", None),
        check_vma=False,
    )
```

```python
import functools

import jax
import jax.numpy as jnp
import numpy as np
from jax import lax
from jax.experimental import pallas as pl
from jax.experimental.pallas import tpu as pltpu
from jax.sharding import PartitionSpec as P

MESH = pl.DeviceIdType.MESH
F32 = jnp.float32
BF16 = jnp.bfloat16
C = 384
T = 16


def one_hot(rows, cols, pairs):
    out = np.zeros((rows, cols), np.float32)
    for r, c in pairs:
        out[r, c] = 1.0
    return out


def moves():
    split = one_hot(256, 256, [
        ((4 * s + c) * 16 + 4 * k + q, (4 * k + c) * 16 + 4 * q + s)
        for s in range(4) for c in range(4) for k in range(4) for q in range(4)])
    edges = one_hot(128, 256, [(m, 4 * m) for m in range(64)] + [(64 + m, 4 * m + 3) for m in range(64)])
    edges_far = one_hot(32, 48, [(m, 4 * m) for m in range(12)] + [(16 + m, 4 * m + 3) for m in range(12)])

    def shift(rows, total, step):
        edge = 0 if step < 0 else 3
        return one_hot(4 * rows, total, [
            (4 * m + q, 4 * rows + m if q == edge else 4 * m + q + step) for m in range(rows) for q in range(4)])

    join = one_hot(128, 128, [
        ((4 * k + c) * 16 + 4 * q + s, (4 * s + c) * 8 + 4 * k + q)
        for s in range(4) for c in range(4) for k in range(2) for q in range(4)])
    parts = (split, edges, edges_far, shift(64, 320, -1), shift(64, 320, 1), shift(12, 64, -1), shift(12, 64, 1), join)
    return jnp.asarray(np.concatenate([np.pad(v, ((0, 0), (0, 384 - v.shape[1]))) for v in parts]), BF16)


def dot(a, b):
    return lax.dot_general(a, b, (((1,), (0,)), ((), ())), preferred_element_type=F32)


def dot_t(a, b):
    return lax.dot_general(a, b, (((1,), (1,)), ((), ())), preferred_element_type=F32)


ROOT = 0.7978845608028654


def gelu_parts(x):
    square = x * x
    t = jnp.tanh(ROOT * (x + 0.044715 * (x * square)))
    half = 0.5 * (1.0 + t)
    slope = half + 0.5 * x * (1.0 - t * t) * (ROOT * (1.0 + 3 * 0.044715 * square))
    return x * half, slope


def kernel(obs_h, base_h, cot_h, w1_h, b1_h, w2_h, b2_h, moves_h,
           out_ref,
           table, b1_ref, b2_ref, obs, base, cot, snd, w1, w2, x, ct, h, hl, hr, a, al, ar, f, nl, nr, ml, mr, pk, pkf,
           qs, qf, slope, adj, pre, back,
           ls, ws, wr, as_, ar_, es, er, fs, fr, os_, or_, near_up, near_down, mid_up, mid_down, wide_up, wide_down):
    p = lax.axis_index("path")
    lon = lax.axis_index("lon")
    lat = lax.axis_index("lat")
    me = lon % T
    zhi = lon // T
    has_l = lat > 0
    has_r = lat < 7

    z = zhi * 8 + lat
    across = {"lon": (lon + T) % (2 * T)}

    def along(step):
        there = (z + step + 16) % 16
        return {"lon": (there // 8) * T + me, "lat": there % 8}

    loads = [pltpu.make_async_copy(src, dst, ls.at[i]) for i, (src, dst) in enumerate(
        ((obs_h, obs), (base_h, base), (cot_h, cot)))]
    half = pl.ds(pl.multiple_of(p * 192, 64), 192)
    own_w = [pltpu.make_async_copy(src, dst.at[:, half, :], ls.at[3 + i]) for i, (src, dst) in enumerate(
        ((w1_h, w1), (w2_h, w2)))]
    more = [pltpu.make_async_copy(src, dst, ls.at[5 + i]) for i, (src, dst) in enumerate(
        ((moves_h, table), (b1_h, b1_ref), (b2_h, b2_ref)))]

    barrier = pltpu.get_barrier_semaphore()

    def greet(**where):
        pl.semaphore_signal(barrier, inc=1, device_id=where, device_id_type=MESH)

    for o in range(1, T):
        greet(lon=zhi * T + (me + o) % T)
    greet(path=1 - p)
    greet(**along(1))
    greet(**along(-1))

    for copy in loads + more + own_w:
        copy.start()

    starts = np.cumsum([0, 256, 128, 32, 256, 256, 48, 48])
    split_ref, edges_ref, edges_far_ref, minus_ref, plus_ref, minus_far_ref, plus_far_ref, join_ref = (
        table.at[int(first):int(first) + size, :width] for first, size, width in zip(
            starts, (256, 128, 32, 256, 256, 48, 48, 128), (256, 256, 48, 384, 384, 128, 128, 128)))

    outside = 2 + 17 * zhi
    past = 19 * (1 - zhi)
    blank = jnp.zeros((16, C), BF16)
    for ref in (h, hl, hr, a, al, ar):
        ref[outside] = blank
    for ref in (nl, nr, ml, mr):
        ref[0] = blank
        ref[5] = blank
    for t in (0, 1, 2, 19, 20, 21):
        f[t] = blank
    for j in range(3):
        qs[j, :64] = jnp.zeros((64, C), F32)
        qs[j, 320:] = jnp.zeros((64, C), F32)

    @pl.when(jnp.logical_not(has_l))
    def _():
        for ref in (hl, al, nl, ml):
            ref[...] = jnp.zeros(ref.shape, BF16)

    @pl.when(jnp.logical_not(has_r))
    def _():
        for ref in (hr, ar, nr, mr):
            ref[...] = jnp.zeros(ref.shape, BF16)

    for copy in loads + more:
        copy.wait()
    low = base[...].astype(F32)
    mix = (p.astype(F32) + 0.5) / 2
    field = (low + mix * (obs[...].astype(F32) - low)).astype(BF16)
    snd[0] = dot(split_ref[...], field.reshape(256, C)).astype(BF16).reshape(T, 16, C)
    snd[1] = dot(split_ref[...], cot[...].reshape(256, C)).astype(BF16).reshape(T, 16, C)

    pl.semaphore_wait(barrier, 18)

    def remote(src, dst, send_sem, recv_sem, where):
        return pltpu.make_async_remote_copy(
            src_ref=src, dst_ref=dst, send_sem=send_sem, recv_sem=recv_sem, device_id=where, device_id_type=MESH)

    def spread(which, o):
        d = (me + o) % T
        dst = (x, ct)[which].at[3 + me]
        return remote(snd.at[which, d], dst, as_.at[which, o], ar_.at[which, o], {"lon": zhi * T + d})

    def gathered(which, o):
        s = (me + T - o) % T
        dst = (x, ct)[which].at[3 + s]
        return remote(snd.at[which, s], dst, as_.at[which, o], ar_.at[which, o], {"lon": zhi * T + s})

    for o in range(1, T):
        spread(0, o).start()
    push_w = [remote(src, dst.at[:, half, :], ws.at[i], wr.at[i], {"path": 1 - p})
              for i, (src, dst) in enumerate(((w1_h, w1), (w2_h, w2)))]
    push_w[0].start()
    x[3 + me] = snd[0, me]
    ct[3 + me] = snd[1, me]

    for step, up, down in ((1, near_up, near_down), (2, mid_up, mid_down), (4, wide_up, wide_down)):
        pl.semaphore_signal(up, inc=1, device_id=along(step), device_id_type=MESH)
        pl.semaphore_signal(down, inc=1, device_id=along(-step), device_id_type=MESH)
        pl.semaphore_wait(up, 1)
        pl.semaphore_wait(down, 1)

    def seam(slot, coming=False):
        side = 1 - zhi if coming else zhi
        ref, base, at, count = ((x, 16 - 13 * zhi, 19 * side, 3), (ct, 17 - 14 * zhi, 1 + 18 * side, 2))[slot]
        return remote(ref.at[pl.ds(base, count)], ref.at[pl.ds(at, count)], fs.at[slot], fr.at[slot], across)

    def right_going(stage, src, dst):
        return remote(src, dst, es.at[stage, 0], er.at[stage, 0], {"lat": lat + 1})

    def left_going(stage, src, dst):
        return remote(src, dst, es.at[stage, 1], er.at[stage, 1], {"lat": lat - 1})

    sent = []

    def give(stage, left_src, right_src, at_left, at_right):
        @pl.when(has_r)
        def _():
            right_going(stage, right_src, at_left).start()

        @pl.when(has_l)
        def _():
            left_going(stage, left_src, at_right).start()

        sent.append((stage, left_src, right_src, at_left, at_right))

    def take(stage):
        left_src, right_src, at_left, at_right = next(v[1:] for v in sent if v[0] == stage)

        @pl.when(has_l)
        def _():
            right_going(stage, right_src, at_left).wait_recv()

        @pl.when(has_r)
        def _():
            left_going(stage, left_src, at_right).wait_recv()

    def give_block(stage, main, left, right, start, count):
        window = pl.ds(start, count)
        give(stage, main.at[window], main.at[window], left.at[window], right.at[window])

    inner = pl.ds(3, 16)
    beyond = pl.ds(past, 3)
    edge = 5 * (1 - zhi)

    def give_edges(stage, main, left, right, layer):
        pk[layer] = dot(edges_ref[...], main[inner].reshape(256, C)).astype(BF16).reshape(8, 16, C)
        give(stage, pk.at[layer, pl.ds(0, 4)], pk.at[layer, pl.ds(4, 4)], left.at[pl.ds(1, 4)], right.at[pl.ds(1, 4)])

    def give_far_edges(stage, main, left, right, layer):
        pkf[layer] = dot(edges_far_ref[...], main[beyond].reshape(48, C)).astype(BF16).reshape(2, 16, C)
        give(stage, pkf.at[layer, pl.ds(0, 1)], pkf.at[layer, pl.ds(1, 1)],
             left.at[pl.ds(edge, 1)], right.at[pl.ds(edge, 1)])

    far_rows = pl.ds(pl.multiple_of(16 * (1 + past), 16), 48)

    def centre(main):
        qs[1, 64:320] = main[inner].reshape(256, C).astype(F32)

    def centre_far(main):
        qs[1, far_rows] = main[beyond].reshape(48, C).astype(F32)

    def sides(main, left, right):
        whole = main[inner].reshape(256, C)
        for j, move, outer in ((0, minus_ref, left), (2, plus_ref, right)):
            qs[j, 64:320] = dot(move[:, :256], whole) + dot(move[:, 256:320], outer[pl.ds(1, 4)].reshape(64, C))

    def sides_far(main, left, right):
        whole = main[beyond].reshape(48, C)
        for j, move, outer in ((0, minus_far_ref, left), (2, plus_far_ref, right)):
            qs[j, far_rows] = dot(move[:, :48], whole) + dot(move[:, 48:64], outer[edge])

    def near_conv(ref, first, rows, weights, forward, columns):
        total = jnp.zeros((rows, C), F32)
        sign = 1 if forward else -1
        for j in columns:
            for i in (-1, 0, 1):
                window = ref[1 + sign * j, pl.ds(first + 4 * sign * i, rows), :].astype(BF16)
                total = total + (dot if forward else dot_t)(window, weights[3 * (i + 1) + j + 1])
        return total

    def far_conv(parts, start, count, weights, forward, columns):
        total = jnp.zeros((16 * count, C), F32)
        sign = 1 if forward else -1
        for j in columns:
            for i in (-1, 0, 1):
                window = parts[1 + sign * j][pl.ds(start + sign * i, count)].reshape(16 * count, C)
                total = total + (dot if forward else dot_t)(window, weights[3 * (i + 1) + j + 1])
        return total

    for o in range(1, T):
        gathered(0, o).wait_recv()

    seam(0).start()
    give_edges(0, x, nl, nr, 0)
    for o in range(1, T):
        spread(1, o).start()
    push_w[1].start()
    centre(x)
    own_w[0].wait()
    push_w[0].wait_recv()
    total = near_conv(qs, 64, 256, w1, True, (0,))
    take(0)
    sides(x, nl, nr)
    act, der = gelu_parts(total + near_conv(qs, 64, 256, w1, True, (-1, 1)) + b1_ref[...])
    slope[inner] = der.reshape(16, 16, C)
    h[inner] = (x[inner].reshape(256, C).astype(F32) + act).astype(BF16).reshape(16, 16, C)
    give_block(2, h, hl, hr, 3 + 8 * zhi, 8)
    give_block(8, h, hl, hr, 11 - 7 * zhi, 7)

    for o in range(1, T):
        gathered(1, o).wait_recv()
    seam(1).start()
    own_w[1].wait()
    push_w[1].wait_recv()
    seam(0, True).wait_recv()
    give_far_edges(1, x, nl, nr, 0)

    def second_forward(start, count, stage):
        window = pl.ds(start, count)
        total = far_conv((hl, h, hr), start, count, w2, True, (0,))
        take(stage)
        _, der = gelu_parts(total + far_conv((hl, h, hr), start, count, w2, True, (-1, 1)) + b2_ref[...])
        a[window] = (der * ct[window].reshape(16 * count, C).astype(F32)).astype(BF16).reshape(count, 16, C)

    early = 3 + 9 * zhi
    second_forward(early, 7, 2)
    give_block(4, a, al, ar, early, 7)
    centre_far(x)
    late = 18 * (1 - zhi)
    rows = pl.ds(pl.multiple_of(16 * late, 16), 96)
    qf[1] = qs[1, rows]
    total = near_conv(qf, 16, 64, w1, True, (0,))
    take(1)
    sides_far(x, nl, nr)
    for j in (0, 2):
        qf[j] = qs[j, rows]
    act, der = gelu_parts(total + near_conv(qf, 16, 64, w1, True, (-1, 1)) + b1_ref[...])
    window = pl.ds(late, 4)
    slope[window] = der.reshape(4, 16, C)
    h[window] = (x[window].reshape(64, C).astype(F32) + act).astype(BF16).reshape(4, 16, C)
    give_block(3, h, hl, hr, late, 4)

    early = 10 - 5 * zhi
    second_forward(early, 7, 8)
    give_block(9, a, al, ar, early, 7)

    seam(1, True).wait_recv()
    late = 17 - 16 * zhi
    second_forward(late, 4, 3)
    give_block(5, a, al, ar, late, 4)

    def second_adjoint(start, count, stage):
        window = pl.ds(start, count)
        total = ct[window].reshape(16 * count, C).astype(F32) + far_conv((al, a, ar), start, count, w2, False, (0,))
        take(stage)
        hidden_adj = total + far_conv((al, a, ar), start, count, w2, False, (-1, 1))
        adj[window] = hidden_adj.reshape(count, 16, C)
        f[window] = (slope[window].reshape(16 * count, C) * hidden_adj).astype(BF16).reshape(count, 16, C)

    second_adjoint(3 + 10 * zhi, 6, 4)
    second_adjoint(9 - 3 * zhi, 7, 9)
    second_adjoint(16 - 14 * zhi, 4, 5)

    give_edges(6, f, ml, mr, 1)
    give_far_edges(7, f, ml, mr, 1)
    centre(f)
    centre_far(f)
    total = adj[inner].reshape(256, C) + near_conv(qs, 64, 256, w1, False, (0,))
    take(6)
    take(7)
    sides(f, ml, mr)
    sides_far(f, ml, mr)
    total = total + near_conv(qs, 64, 256, w1, False, (-1, 1))
    pre[...] = total.reshape(16, 2, 8, C).astype(BF16)

    def collect(o, core):
        d = (me + o) % T
        return remote(pre.at[d, core], back.at[p, me], os_.at[o, core], or_.at[o, p],
                      {"lon": zhi * T + d, "path": core})

    def collected(o, core):
        s = (me + T - o) % T
        return remote(pre.at[s, p], back.at[core, s], os_.at[o, core], or_.at[o, core],
                      {"lon": zhi * T + s, "path": core})

    for o in range(T):
        for core in (p, 1 - p)[0 if o else 1:]:
            collect(o, core).start()
    back[p, me] = pre[me, p]
    for stage, left_src, right_src, at_left, at_right in sent:
        @pl.when(has_r)
        def _():
            right_going(stage, right_src, at_left).wait_send()

        @pl.when(has_l)
        def _():
            left_going(stage, left_src, at_right).wait_send()

    seam(0).wait_send()
    seam(1).wait_send()
    for o in range(1, T):
        for which in (0, 1):
            spread(which, o).wait_send()
    for copy in push_w:
        copy.wait_send()
    for o in range(T):
        for core in (p, 1 - p)[0 if o else 1:]:
            collected(o, core).wait_recv()
    total = dot(join_ref[...], back[0].reshape(128, C)) + dot(join_ref[...], back[1].reshape(128, C))
    rows = pl.ds(p * 8, 8)
    diff = obs[rows].astype(F32) - base[rows].astype(F32)
    out_ref[...] = (diff * total.reshape(8, 16, C) / 2).astype(BF16)
    for o in range(T):
        for core in (p, 1 - p)[0 if o else 1:]:
            collect(o, core).wait_send()


def shards(observed, baseline, cotangent, first_weight, first_bias, second_weight, second_bias):
    hbm = pl.BlockSpec(memory_space=pl.ANY)
    vmem = pl.BlockSpec(memory_space=pltpu.VMEM)
    tiles = lambda n, dtype=BF16: pltpu.VMEM((n, 16, C), dtype)
    ext = tiles(22)
    dma = pltpu.SemaphoreType.DMA
    constants = moves()
    return pl.pallas_call(
        kernel,
        out_shape=jax.ShapeDtypeStruct((8, 16, C), BF16),
        in_specs=[hbm] * 8,
        out_specs=vmem,
        scratch_shapes=[
            pltpu.VMEM(constants.shape, BF16), pltpu.VMEM((1, C), F32), pltpu.VMEM((1, C), F32),
            tiles(16), tiles(16), tiles(16), pltpu.VMEM((2, 16, 16, C), BF16),
            pltpu.VMEM((9, C, C), BF16), pltpu.VMEM((9, C, C), BF16),
            ext, ext, ext, ext, ext, ext, ext, ext, ext, tiles(6), tiles(6), tiles(6), tiles(6),
            pltpu.VMEM((2, 8, 16, C), BF16), pltpu.VMEM((2, 2, 16, C), BF16),
            pltpu.VMEM((3, 384, C), F32), pltpu.VMEM((3, 96, C), F32),
            tiles(22, F32), tiles(22, F32),
            pltpu.VMEM((16, 2, 8, C), BF16), pltpu.VMEM((2, 16, 8, C), BF16),
            dma((8,)), dma((2,)), dma((2,)), dma((2, T)), dma((2, T)), dma((10, 2)), dma((10, 2)), dma((2,)), dma((2,)),
            dma((T, 2)), dma((T, 2)), *[pltpu.SemaphoreType.REGULAR] * 6,
        ],
        compiler_params=pltpu.CompilerParams(collective_id=0, has_side_effects=True),
    )(observed, baseline, cotangent, first_weight, first_bias.reshape(1, C), second_weight,
      second_bias.reshape(1, C), constants)


def solution(mesh):
    placed = (
        P("lon", "lat", None),
        P("lon", "lat", None),
        P("lon", "lat", None),
        P(None, "path", None),
        P(),
        P(None, "path", None),
        P(),
    )
    return jax.shard_map(
        shards,
        mesh=mesh,
        in_specs=placed,
        out_specs=P(("lon", "path"), "lat", None),
        check_vma=False,
    )
```

```python
import functools

import jax
import jax.numpy as jnp
import numpy as np
from jax import lax
from jax.experimental import pallas as pl
from jax.experimental.pallas import tpu as pltpu
from jax.sharding import PartitionSpec as P

MESH = pl.DeviceIdType.MESH
F32 = jnp.float32
BF16 = jnp.bfloat16
C = 384
T = 16


def one_hot(rows, cols, pairs):
    out = np.zeros((rows, cols), np.float32)
    for r, c in pairs:
        out[r, c] = 1.0
    return out


def moves():
    split = one_hot(256, 256, [
        ((4 * s + c) * 16 + 4 * k + q, (4 * k + c) * 16 + 4 * q + s)
        for s in range(4) for c in range(4) for k in range(4) for q in range(4)])
    edges = one_hot(128, 256, [(m, 4 * m) for m in range(64)] + [(64 + m, 4 * m + 3) for m in range(64)])
    edges_far = one_hot(32, 48, [(m, 4 * m) for m in range(12)] + [(16 + m, 4 * m + 3) for m in range(12)])

    def shift(rows, total, step):
        edge = 0 if step < 0 else 3
        return one_hot(4 * rows, total, [
            (4 * m + q, 4 * rows + m if q == edge else 4 * m + q + step) for m in range(rows) for q in range(4)])

    join = one_hot(128, 128, [
        ((4 * k + c) * 16 + 4 * q + s, (4 * s + c) * 8 + 4 * k + q)
        for s in range(4) for c in range(4) for k in range(2) for q in range(4)])
    parts = (split, edges, edges_far, shift(64, 320, -1), shift(64, 320, 1), shift(12, 64, -1), shift(12, 64, 1), join)
    return jnp.asarray(np.concatenate([np.pad(v, ((0, 0), (0, 384 - v.shape[1]))) for v in parts]), BF16)


def dot(a, b):
    return lax.dot_general(a, b, (((1,), (0,)), ((), ())), preferred_element_type=F32)


def dot_t(a, b):
    return lax.dot_general(a, b, (((1,), (1,)), ((), ())), preferred_element_type=F32)


ROOT = 0.7978845608028654


def gelu_parts(x):
    square = x * x
    t = jnp.tanh(ROOT * (x + 0.044715 * (x * square)))
    half = 0.5 * (1.0 + t)
    slope = half + 0.5 * x * (1.0 - t * t) * (ROOT * (1.0 + 3 * 0.044715 * square))
    return x * half, slope


def kernel(obs_h, base_h, cot_h, w1_h, b1_h, w2_h, b2_h, moves_h,
           out_ref,
           table, b1_ref, b2_ref, obs, base, cot, snd, w1, w2, x, ct, h, hl, hr, a, al, ar, f, nl, nr, ml, mr, pk, pkf,
           qs, qf, slope, adj, pre, back,
           ls, ws, wr, as_, ar_, es, er, fs, fr, os_, or_, near_up, near_down, mid_up, mid_down, wide_up, wide_down):
    p = lax.axis_index("path")
    lon = lax.axis_index("lon")
    lat = lax.axis_index("lat")
    me = lon % T
    zhi = lon // T
    has_l = lat > 0
    has_r = lat < 7

    z = zhi * 8 + lat
    across = {"lon": (lon + T) % (2 * T)}

    def along(step):
        there = (z + step + 16) % 16
        return {"lon": (there // 8) * T + me, "lat": there % 8}

    loads = [pltpu.make_async_copy(src, dst, ls.at[i]) for i, (src, dst) in enumerate(
        ((obs_h, obs), (base_h, base), (cot_h, cot)))]
    half = pl.ds(pl.multiple_of(p * 192, 64), 192)
    own_w = [pltpu.make_async_copy(src, dst.at[:, half, :], ls.at[3 + i]) for i, (src, dst) in enumerate(
        ((w1_h, w1), (w2_h, w2)))]
    more = [pltpu.make_async_copy(src, dst, ls.at[5 + i]) for i, (src, dst) in enumerate(
        ((moves_h, table), (b1_h, b1_ref), (b2_h, b2_ref)))]

    barrier = pltpu.get_barrier_semaphore()

    def greet(**where):
        pl.semaphore_signal(barrier, inc=1, device_id=where, device_id_type=MESH)

    for o in range(1, T):
        greet(lon=zhi * T + (me + o) % T)
    greet(path=1 - p)
    greet(**along(1))
    greet(**along(-1))

    for copy in loads + more + own_w:
        copy.start()

    starts = np.cumsum([0, 256, 128, 32, 256, 256, 48, 48])
    split_ref, edges_ref, edges_far_ref, minus_ref, plus_ref, minus_far_ref, plus_far_ref, join_ref = (
        table.at[int(first):int(first) + size, :width] for first, size, width in zip(
            starts, (256, 128, 32, 256, 256, 48, 48, 128), (256, 256, 48, 384, 384, 128, 128, 128)))

    outside = 2 + 17 * zhi
    past = 19 * (1 - zhi)
    blank = jnp.zeros((16, C), BF16)
    for ref in (h, hl, hr, a, al, ar):
        ref[outside] = blank
    for ref in (nl, nr, ml, mr):
        ref[0] = blank
        ref[5] = blank
    for t in (0, 1, 2, 19, 20, 21):
        f[t] = blank
    for j in range(3):
        qs[j, :64] = jnp.zeros((64, C), F32)
        qs[j, 320:] = jnp.zeros((64, C), F32)

    @pl.when(jnp.logical_not(has_l))
    def _():
        for ref in (hl, al, nl, ml):
            ref[...] = jnp.zeros(ref.shape, BF16)

    @pl.when(jnp.logical_not(has_r))
    def _():
        for ref in (hr, ar, nr, mr):
            ref[...] = jnp.zeros(ref.shape, BF16)

    for copy in loads + more:
        copy.wait()
    low = base[...].astype(F32)
    mix = (p.astype(F32) + 0.5) / 2
    field = (low + mix * (obs[...].astype(F32) - low)).astype(BF16)
    snd[0] = dot(split_ref[...], field.reshape(256, C)).astype(BF16).reshape(T, 16, C)
    snd[1] = dot(split_ref[...], cot[...].reshape(256, C)).astype(BF16).reshape(T, 16, C)

    pl.semaphore_wait(barrier, 18)

    def remote(src, dst, send_sem, recv_sem, where):
        return pltpu.make_async_remote_copy(
            src_ref=src, dst_ref=dst, send_sem=send_sem, recv_sem=recv_sem, device_id=where, device_id_type=MESH)

    def spread(which, o):
        d = (me + o) % T
        dst = (x, ct)[which].at[3 + me]
        return remote(snd.at[which, d], dst, as_.at[which, o], ar_.at[which, o], {"lon": zhi * T + d})

    def gathered(which, o):
        s = (me + T - o) % T
        dst = (x, ct)[which].at[3 + s]
        return remote(snd.at[which, s], dst, as_.at[which, o], ar_.at[which, o], {"lon": zhi * T + s})

    for o in range(1, T):
        spread(0, o).start()
    push_w = [remote(src, dst.at[:, half, :], ws.at[i], wr.at[i], {"path": 1 - p})
              for i, (src, dst) in enumerate(((w1_h, w1), (w2_h, w2)))]
    push_w[0].start()
    x[3 + me] = snd[0, me]
    ct[3 + me] = snd[1, me]

    for step, up, down in ((1, near_up, near_down), (2, mid_up, mid_down), (4, wide_up, wide_down)):
        pl.semaphore_signal(up, inc=1, device_id=along(step), device_id_type=MESH)
        pl.semaphore_signal(down, inc=1, device_id=along(-step), device_id_type=MESH)
        pl.semaphore_wait(up, 1)
        pl.semaphore_wait(down, 1)

    def seam(slot, coming=False):
        side = 1 - zhi if coming else zhi
        ref, base, at, count = ((x, 16 - 13 * zhi, 19 * side, 3), (ct, 17 - 14 * zhi, 1 + 18 * side, 2))[slot]
        return remote(ref.at[pl.ds(base, count)], ref.at[pl.ds(at, count)], fs.at[slot], fr.at[slot], across)

    def right_going(stage, src, dst):
        return remote(src, dst, es.at[stage, 0], er.at[stage, 0], {"lat": lat + 1})

    def left_going(stage, src, dst):
        return remote(src, dst, es.at[stage, 1], er.at[stage, 1], {"lat": lat - 1})

    sent = []

    def give(stage, left_src, right_src, at_left, at_right):
        @pl.when(has_r)
        def _():
            right_going(stage, right_src, at_left).start()

        @pl.when(has_l)
        def _():
            left_going(stage, left_src, at_right).start()

        sent.append((stage, left_src, right_src, at_left, at_right))

    def take(stage):
        left_src, right_src, at_left, at_right = next(v[1:] for v in sent if v[0] == stage)

        @pl.when(has_l)
        def _():
            right_going(stage, right_src, at_left).wait_recv()

        @pl.when(has_r)
        def _():
            left_going(stage, left_src, at_right).wait_recv()

    def give_block(stage, main, left, right, start, count):
        window = pl.ds(start, count)
        give(stage, main.at[window], main.at[window], left.at[window], right.at[window])

    inner = pl.ds(3, 16)
    beyond = pl.ds(past, 3)
    edge = 5 * (1 - zhi)

    def give_edges(stage, main, left, right, layer):
        pk[layer] = dot(edges_ref[...], main[inner].reshape(256, C)).astype(BF16).reshape(8, 16, C)
        give(stage, pk.at[layer, pl.ds(0, 4)], pk.at[layer, pl.ds(4, 4)], left.at[pl.ds(1, 4)], right.at[pl.ds(1, 4)])

    def give_far_edges(stage, main, left, right, layer):
        pkf[layer] = dot(edges_far_ref[...], main[beyond].reshape(48, C)).astype(BF16).reshape(2, 16, C)
        give(stage, pkf.at[layer, pl.ds(0, 1)], pkf.at[layer, pl.ds(1, 1)],
             left.at[pl.ds(edge, 1)], right.at[pl.ds(edge, 1)])

    far_rows = pl.ds(pl.multiple_of(16 * (1 + past), 16), 48)

    def centre(main):
        qs[1, 64:320] = main[inner].reshape(256, C).astype(F32)

    def centre_far(main):
        qs[1, far_rows] = main[beyond].reshape(48, C).astype(F32)

    def sides(main, left, right):
        whole = main[inner].reshape(256, C)
        for j, move, outer in ((0, minus_ref, left), (2, plus_ref, right)):
            qs[j, 64:320] = dot(move[:, :256], whole) + dot(move[:, 256:320], outer[pl.ds(1, 4)].reshape(64, C))

    def sides_far(main, left, right):
        whole = main[beyond].reshape(48, C)
        for j, move, outer in ((0, minus_far_ref, left), (2, plus_far_ref, right)):
            qs[j, far_rows] = dot(move[:, :48], whole) + dot(move[:, 48:64], outer[edge])

    def near_conv(ref, first, rows, weights, forward, columns):
        total = jnp.zeros((rows, C), F32)
        sign = 1 if forward else -1
        for j in columns:
            for i in (-1, 0, 1):
                window = ref[1 + sign * j, pl.ds(first + 4 * sign * i, rows), :].astype(BF16)
                total = total + (dot if forward else dot_t)(window, weights[3 * (i + 1) + j + 1])
        return total

    def far_conv(parts, start, count, weights, forward, columns):
        total = jnp.zeros((16 * count, C), F32)
        sign = 1 if forward else -1
        for j in columns:
            for i in (-1, 0, 1):
                window = parts[1 + sign * j][pl.ds(start + sign * i, count)].reshape(16 * count, C)
                total = total + (dot if forward else dot_t)(window, weights[3 * (i + 1) + j + 1])
        return total

    for o in range(1, T):
        gathered(0, o).wait_recv()

    seam(0).start()
    give_edges(0, x, nl, nr, 0)
    for o in range(1, T):
        spread(1, o).start()
    push_w[1].start()
    centre(x)
    own_w[0].wait()
    push_w[0].wait_recv()
    total = near_conv(qs, 64, 256, w1, True, (0,))
    take(0)
    sides(x, nl, nr)
    act, der = gelu_parts(total + near_conv(qs, 64, 256, w1, True, (-1, 1)) + b1_ref[...])
    slope[inner] = der.reshape(16, 16, C)
    h[inner] = (x[inner].reshape(256, C).astype(F32) + act).astype(BF16).reshape(16, 16, C)
    give_block(2, h, hl, hr, 3 + 8 * zhi, 8)
    give_block(8, h, hl, hr, 11 - 7 * zhi, 7)

    for o in range(1, T):
        gathered(1, o).wait_recv()
    seam(1).start()
    own_w[1].wait()
    push_w[1].wait_recv()
    seam(0, True).wait_recv()
    give_far_edges(1, x, nl, nr, 0)

    def second_forward(start, count, stage):
        window = pl.ds(start, count)
        total = far_conv((hl, h, hr), start, count, w2, True, (0,))
        take(stage)
        _, der = gelu_parts(total + far_conv((hl, h, hr), start, count, w2, True, (-1, 1)) + b2_ref[...])
        a[window] = (der * ct[window].reshape(16 * count, C).astype(F32)).astype(BF16).reshape(count, 16, C)

    early = 3 + 9 * zhi
    second_forward(early, 7, 2)
    first = early
    centre_far(x)
    late = 18 * (1 - zhi)
    rows = pl.ds(pl.multiple_of(16 * late, 16), 96)
    qf[1] = qs[1, rows]
    total = near_conv(qf, 16, 64, w1, True, (0,))
    take(1)
    sides_far(x, nl, nr)
    for j in (0, 2):
        qf[j] = qs[j, rows]
    act, der = gelu_parts(total + near_conv(qf, 16, 64, w1, True, (-1, 1)) + b1_ref[...])
    window = pl.ds(late, 4)
    slope[window] = der.reshape(4, 16, C)
    h[window] = (x[window].reshape(64, C).astype(F32) + act).astype(BF16).reshape(4, 16, C)
    give_block(3, h, hl, hr, late, 4)
    give_block(4, a, al, ar, first, 7)

    early = 10 - 5 * zhi
    second_forward(early, 7, 8)
    give_block(9, a, al, ar, early, 7)

    seam(1, True).wait_recv()
    late = 17 - 16 * zhi
    second_forward(late, 4, 3)
    give_block(5, a, al, ar, late, 4)

    def second_adjoint(start, count, stage):
        window = pl.ds(start, count)
        total = ct[window].reshape(16 * count, C).astype(F32) + far_conv((al, a, ar), start, count, w2, False, (0,))
        take(stage)
        hidden_adj = total + far_conv((al, a, ar), start, count, w2, False, (-1, 1))
        adj[window] = hidden_adj.reshape(count, 16, C)
        f[window] = (slope[window].reshape(16 * count, C) * hidden_adj).astype(BF16).reshape(count, 16, C)

    second_adjoint(3 + 10 * zhi, 6, 4)
    second_adjoint(9 - 3 * zhi, 7, 9)
    second_adjoint(16 - 14 * zhi, 4, 5)

    give_edges(6, f, ml, mr, 1)
    give_far_edges(7, f, ml, mr, 1)
    centre(f)
    centre_far(f)
    total = adj[inner].reshape(256, C) + near_conv(qs, 64, 256, w1, False, (0,))
    take(6)
    take(7)
    sides(f, ml, mr)
    sides_far(f, ml, mr)
    total = total + near_conv(qs, 64, 256, w1, False, (-1, 1))
    pre[...] = total.reshape(16, 2, 8, C).astype(BF16)

    def collect(o, core):
        d = (me + o) % T
        return remote(pre.at[d, core], back.at[p, me], os_.at[o, core], or_.at[o, p],
                      {"lon": zhi * T + d, "path": core})

    def collected(o, core):
        s = (me + T - o) % T
        return remote(pre.at[s, p], back.at[core, s], os_.at[o, core], or_.at[o, core],
                      {"lon": zhi * T + s, "path": core})

    for o in range(T):
        for core in (p, 1 - p)[0 if o else 1:]:
            collect(o, core).start()
    back[p, me] = pre[me, p]
    for stage, left_src, right_src, at_left, at_right in sent:
        @pl.when(has_r)
        def _():
            right_going(stage, right_src, at_left).wait_send()

        @pl.when(has_l)
        def _():
            left_going(stage, left_src, at_right).wait_send()

    seam(0).wait_send()
    seam(1).wait_send()
    for o in range(1, T):
        for which in (0, 1):
            spread(which, o).wait_send()
    for copy in push_w:
        copy.wait_send()
    for o in range(T):
        for core in (p, 1 - p)[0 if o else 1:]:
            collected(o, core).wait_recv()
    total = dot(join_ref[...], back[0].reshape(128, C)) + dot(join_ref[...], back[1].reshape(128, C))
    rows = pl.ds(p * 8, 8)
    diff = obs[rows].astype(F32) - base[rows].astype(F32)
    out_ref[...] = (diff * total.reshape(8, 16, C) / 2).astype(BF16)
    for o in range(T):
        for core in (p, 1 - p)[0 if o else 1:]:
            collect(o, core).wait_send()


def shards(observed, baseline, cotangent, first_weight, first_bias, second_weight, second_bias):
    hbm = pl.BlockSpec(memory_space=pl.ANY)
    vmem = pl.BlockSpec(memory_space=pltpu.VMEM)
    tiles = lambda n, dtype=BF16: pltpu.VMEM((n, 16, C), dtype)
    ext = tiles(22)
    dma = pltpu.SemaphoreType.DMA
    constants = moves()
    return pl.pallas_call(
        kernel,
        out_shape=jax.ShapeDtypeStruct((8, 16, C), BF16),
        in_specs=[hbm] * 8,
        out_specs=vmem,
        scratch_shapes=[
            pltpu.VMEM(constants.shape, BF16), pltpu.VMEM((1, C), F32), pltpu.VMEM((1, C), F32),
            tiles(16), tiles(16), tiles(16), pltpu.VMEM((2, 16, 16, C), BF16),
            pltpu.VMEM((9, C, C), BF16), pltpu.VMEM((9, C, C), BF16),
            ext, ext, ext, ext, ext, ext, ext, ext, ext, tiles(6), tiles(6), tiles(6), tiles(6),
            pltpu.VMEM((2, 8, 16, C), BF16), pltpu.VMEM((2, 2, 16, C), BF16),
            pltpu.VMEM((3, 384, C), F32), pltpu.VMEM((3, 96, C), F32),
            tiles(22, F32), tiles(22, F32),
            pltpu.VMEM((16, 2, 8, C), BF16), pltpu.VMEM((2, 16, 8, C), BF16),
            dma((8,)), dma((2,)), dma((2,)), dma((2, T)), dma((2, T)), dma((10, 2)), dma((10, 2)), dma((2,)), dma((2,)),
            dma((T, 2)), dma((T, 2)), *[pltpu.SemaphoreType.REGULAR] * 6,
        ],
        compiler_params=pltpu.CompilerParams(collective_id=0, has_side_effects=True),
    )(observed, baseline, cotangent, first_weight, first_bias.reshape(1, C), second_weight,
      second_bias.reshape(1, C), constants)


def solution(mesh):
    placed = (
        P("lon", "lat", None),
        P("lon", "lat", None),
        P("lon", "lat", None),
        P(None, "path", None),
        P(),
        P(None, "path", None),
        P(),
    )
    return jax.shard_map(
        shards,
        mesh=mesh,
        in_specs=placed,
        out_specs=P(("lon", "path"), "lat", None),
        check_vma=False,
    )
```
